32 devices in a mesh: ctx: 16 (over z, y, x), head: 2 (over core).
Axes of the slice: x: 2, y: 2, z: 4, core: 2. Of those that a mesh axis runs over, the one named last changes fastest.
Arguments:
- queries: float32 [8192, 512], P('ctx', 'head'), may hold values from -1024 to 1024
- keys: float32 [8192, 128], P('ctx'), may hold values from -1024 to 1024
- values: float32 [8192, 128], P('ctx'), may hold values from -6 to 6
- cotangent: float32 [8192, 512], P('ctx', 'head'), may hold values from -384 to 384
- source_ids: int32 [8192], P('ctx'), may hold values from 0 to 63
- source_weights: float32 [64], replicated, may hold values from 0.25 to 4
- q_feature: float32 [4, 128, 128], P('head'), may hold values from -4 to 4
- k_feature: float32 [128, 128], replicated, may hold values from -4 to 4
Outputs:
- grad_queries: float32 [8192, 512], P('ctx', 'head')
- grad_keys: float32 [8192, 128], P(('ctx', 'head'))
- grad_values: float32 [8192, 128], P(('ctx', 'head'))
- grad_q_feature: float32 [4, 128, 128], P('head')
- grad_k_feature: float32 [128, 128], replicated
The draws below stay inside these ranges and needn't reach their ends.
All inputs are finite; a program needn't handle non-finite values.
Results may differ from the reference program's by a relative error of at most 0.0015.
Values sent between devices are 32-bit elements; how exact they have to be, the bound alone decides.
No kernel may reach another device: no remote copies, remote signals or barrier semaphores. Data moves between devices by JAX's collectives and lax.ppermute only.
A program may use at most 64 MiB of HBM per device.

```python
import math
import jax
import jax.numpy as jnp
import numpy as np
from jax import lax

D = 128
F = 128
HQ = 4
TOK_DEV = 512
TOKENS = 8192
SOURCES = 64


def feature_table(key, count):
    table = jax.random.normal(key, (count, D, F), jnp.float32)
    return jnp.clip(table, -6.0, 6.0) * (3.0 * D ** (-0.5))


def draw_q_feature(key, part):
    return feature_table(jax.random.fold_in(key, 101), HQ)


def draw_k_feature(key, part):
    return feature_table(jax.random.fold_in(key, 102), 1)[0]


def drawn_rows(key, count_rows, count_heads):
    subkeys = jax.random.split(key, 1)
    base = jnp.clip(jax.random.normal(subkeys[0], (count_rows, count_heads, D), jnp.float32), -6.0, 6.0)
    return base


def draw_queries(key, part):
    return drawn_rows(jax.random.fold_in(key, 201), TOKENS, HQ).reshape(TOKENS, HQ * D)


def draw_keys(key, part):
    return drawn_rows(jax.random.fold_in(key, 202), TOKENS, 1).reshape(TOKENS, D)


def plant(drawn, rng, least, largest):
    shape = drawn.shape
    index_at = [jax.random.randint(jax.random.fold_in(rng, axis), (), 0, shape[axis]) for axis in range(len(shape))]
    drawn = drawn.at[tuple(index_at)].set(least)
    longest = shape.index(max(shape))
    index_at[longest] = (index_at[longest] + 1) % shape[longest]
    return drawn.at[tuple(index_at)].set(largest)


def level_of(stream_key, shape, shards, low, high):
    def one(dim, blocks):
        draws = jax.random.uniform(jax.random.fold_in(jax.random.fold_in(stream_key, 6), dim), (blocks,), jnp.float32, low / len(shards), high / len(shards))
        return jnp.repeat(jnp.exp(draws), shape[dim] // blocks).reshape((-1,) + (1,) * (len(shape) - dim - 1))

    factor_of = one(*shards[0])
    for cut in shards[1:]:
        factor_of = factor_of * one(*cut)
    return factor_of


def rank_table(amount, skew):
    weights = [(1 << 20) // math.isqrt(grade ** skew) + 1 for grade in range(1, amount + 1)]
    deviation = 1 + sum(weights) // (1 << 30)
    return np.cumsum(np.array([max(1, weight // deviation) for weight in weights]))


def skewed_ids(own_key, shape, count, skew):
    listing = rank_table(count, skew)
    lot = jax.random.randint(jax.random.fold_in(own_key, 1), shape, 0, int(listing[count - 1]))
    standing = jnp.searchsorted(jnp.asarray(listing, jnp.int32), lot, side="right")
    return jax.random.permutation(jax.random.fold_in(own_key, 2), count)[standing].astype(jnp.int32)


def normal_values(stream_key, shape, width, limit, pieces=(), kind=jnp.bfloat16):
    result = width * jax.random.normal(stream_key, shape, jnp.float32)
    if pieces:
        result = result * level_of(stream_key, shape, pieces, -0.22, 0.18)
    return jnp.clip(result, -limit, limit).astype(kind)


def setup_inputs(seed: int = 0) -> dict:
    seeds = jax.random.split(jax.random.key(seed), 9)
    queries = draw_queries(jax.random.fold_in(seeds[8], 71), 0)
    keys = draw_keys(jax.random.fold_in(seeds[8], 71), 0)
    values = normal_values(seeds[2], (TOKENS, D), 1.0, 6.0, ((0, 16),), jnp.float32)
    cotangent = normal_values(seeds[3], (TOKENS, HQ * D), 64.0, 384.0, ((0, 16), (1, 2)), jnp.float32)
    source_ids = plant(skewed_ids(seeds[4], (TOKENS,), SOURCES, 2), jax.random.fold_in(seeds[4], 3), 0, SOURCES - 1).astype(jnp.int32)
    source_weights = jnp.clip(jnp.exp(jax.random.uniform(seeds[5], (SOURCES,), jnp.float32, math.log(0.25), math.log(4.0))), 0.25, 4.0)
    q_feature = draw_q_feature(jax.random.fold_in(seeds[8], 71), 0)
    k_feature = draw_k_feature(jax.random.fold_in(seeds[8], 71), 0)
    return {"queries": queries, "keys": keys, "values": values, "cotangent": cotangent, "source_ids": source_ids, "source_weights": source_weights, "q_feature": q_feature, "k_feature": k_feature}


def matmul(left, right):
    return jnp.dot(left, right, precision=lax.Precision.HIGHEST, preferred_element_type=jnp.float32)


def feature_map(inputs, weight):
    logits = matmul(inputs, weight)
    upper = jax.nn.softmax(logits, axis=-1)
    lower = jax.nn.softmax(-logits, axis=-1)
    return jnp.concatenate([upper, lower], axis=-1), upper, lower


def feature_back(inputs, weight, upper, lower, grad_feat):
    half = upper.shape[-1]
    grad_upper = grad_feat[:, :half]
    grad_lower = grad_feat[:, half:]
    grad_logits = upper * (grad_upper - jnp.sum(upper * grad_upper, axis=-1, keepdims=True))
    grad_logits = grad_logits - lower * (grad_lower - jnp.sum(lower * grad_lower, axis=-1, keepdims=True))
    return matmul(grad_logits, weight.T), matmul(inputs.T, grad_logits)


def causal_mask(count):
    row_index = lax.broadcasted_iota(jnp.int32, (count, count), 0)
    col_index = lax.broadcasted_iota(jnp.int32, (count, count), 1)
    return (row_index >= col_index).astype(jnp.float32)


def block_terms(query_feat, key_feat, value_rows, scaled, earlier, earlier_totals):
    lower_mask = causal_mask(query_feat.shape[0])
    scores = matmul(query_feat, key_feat.T) * lower_mask
    numerator = matmul(scores, value_rows) + matmul(query_feat, earlier)
    normalizer = jnp.sum(scores, axis=1) + matmul(query_feat, earlier_totals)
    output = numerator / normalizer[:, None]
    grad_numer = scaled / normalizer[:, None]
    grad_norm = -jnp.sum(scaled * output, axis=1) / normalizer
    grad_scores = (matmul(grad_numer, value_rows.T) + grad_norm[:, None]) * lower_mask
    grad_query = matmul(grad_scores, key_feat) + matmul(grad_numer, earlier.T) + grad_norm[:, None] * earlier_totals[None, :]
    grad_key = matmul(grad_scores.T, query_feat)
    grad_value = matmul(scores.T, grad_numer)
    carried = matmul(query_feat.T, grad_numer)
    carried_totals = matmul(grad_norm[None, :], query_feat)[0]
    return grad_query, grad_key, grad_value, carried, carried_totals


def reference(queries, keys, values, cotangent, source_ids, source_weights, q_feature, k_feature):
    count = queries.shape[0]
    blocks = count // TOK_DEV
    features = 2 * F
    weight = source_weights[source_ids]
    key_feat, key_upper, key_lower = feature_map(keys, k_feature)
    key_blocks = key_feat.reshape(blocks, TOK_DEV, features)
    value_blocks = values.reshape(blocks, TOK_DEV, D)
    grad_keyfeat = jnp.zeros((count, features), jnp.float32)
    grad_vals = jnp.zeros((count, D), jnp.float32)
    carried_all = jnp.zeros((blocks, features, D), jnp.float32)
    carried_tot = jnp.zeros((blocks, features), jnp.float32)
    query_grads = []
    weight_grads = []
    for head in range(HQ):
        query_head = queries[:, head * D:(head + 1) * D]
        query_feat, query_upper, query_lower = feature_map(query_head, q_feature[head])
        scaled = cotangent[:, head * D:(head + 1) * D] * weight[:, None]

        def advance(carry, inputs):
            earlier, earlier_totals = carry
            query_block, key_block, value_block, scaled_block = inputs
            terms = block_terms(query_block, key_block, value_block, scaled_block, earlier, earlier_totals)
            earlier = earlier + matmul(key_block.T, value_block)
            earlier_totals = earlier_totals + jnp.sum(key_block, axis=0)
            return (earlier, earlier_totals), terms

        start_state = (jnp.zeros((features, D), jnp.float32), jnp.zeros((features,), jnp.float32))
        inputs = (query_feat.reshape(blocks, TOK_DEV, features), key_blocks, value_blocks, scaled.reshape(blocks, TOK_DEV, D))
        _, outputs = lax.scan(advance, start_state, inputs)
        grad_query, grad_key, grad_value, carried, carried_totals = outputs
        grad_head, grad_weight = feature_back(query_head, q_feature[head], query_upper, query_lower, grad_query.reshape(count, features))
        query_grads.append(grad_head)
        weight_grads.append(grad_weight)
        grad_keyfeat = grad_keyfeat + grad_key.reshape(count, features)
        grad_vals = grad_vals + grad_value.reshape(count, D)
        carried_all = carried_all + carried
        carried_tot = carried_tot + carried_totals
    later = jnp.flip(jnp.cumsum(jnp.flip(carried_all, 0), axis=0), 0) - carried_all
    later_tot = jnp.flip(jnp.cumsum(jnp.flip(carried_tot, 0), axis=0), 0) - carried_tot
    inter_key = jnp.einsum("bte,bfe->btf", value_blocks, later, precision=lax.Precision.HIGHEST) + later_tot[:, None, :]
    inter_value = jnp.einsum("btf,bfe->bte", key_blocks, later, precision=lax.Precision.HIGHEST)
    grad_keyfeat = grad_keyfeat + inter_key.reshape(count, features)
    grad_vals = grad_vals + inter_value.reshape(count, D)
    grad_keys, grad_kweight = feature_back(keys, k_feature, key_upper, key_lower, grad_keyfeat)
    grad_queries = jnp.concatenate(query_grads, axis=1)
    grad_qweight = jnp.stack(weight_grads, axis=0)
    return grad_queries, grad_keys, grad_vals, grad_qweight, grad_kweight
```

```python
import functools

import jax
import jax.numpy as jnp
from jax import lax
from jax.experimental import pallas as pl
from jax.experimental.pallas import tpu as pltpu
from jax.sharding import PartitionSpec as P


F32 = jnp.float32
BF16 = jnp.bfloat16
NN = ((1,), (0,))
NT = ((1,), (1,))
TN = ((0,), (0,))


def split(x):
    high = x.astype(BF16)
    return high, (x - high.astype(F32)).astype(BF16)


def joined(pair):
    return pair[0].astype(F32) + pair[1].astype(F32)


def raw_dot(a, b, dims):
    return lax.dot_general(a, b, (dims, ((), ())), preferred_element_type=F32)


def dot3(a, b, dims):
    return raw_dot(a[0], b[0], dims) + (raw_dot(a[0], b[1], dims) + raw_dot(a[1], b[0], dims))


def dot_exact(a, b, dims):
    return lax.dot_general(
        a, b, (dims, ((), ())), precision=lax.Precision.HIGHEST, preferred_element_type=F32
    )


def softmaxes(logits):
    upper = jnp.exp(logits - jnp.max(logits, axis=-1, keepdims=True))
    lower = jnp.exp(jnp.min(logits, axis=-1, keepdims=True) - logits)
    return (
        upper / jnp.sum(upper, axis=-1, keepdims=True),
        lower / jnp.sum(lower, axis=-1, keepdims=True),
    )


def logit_grad(features, grad):
    half = features.shape[1] // 2
    upper, lower = features[:, :half], features[:, half:]
    a, b = grad[:, :half], grad[:, half:]
    up = upper * (a - jnp.sum(upper * a, axis=-1, keepdims=True))
    return up - lower * (b - jnp.sum(lower * b, axis=-1, keepdims=True))


def digits_of(count):
    found, base = [], 1
    while base < count:
        radix = 4 if (count // base) % 4 == 0 else 2
        found.append((base, radix))
        base *= radix
    return found


def exchange(values, axis, base, radix):
    count = lax.axis_size(axis)
    received = []
    for m in range(1, radix):
        value = values[m - 1] if isinstance(values, (list, tuple)) else values
        received.append(lax.ppermute(value, axis, [(i, i ^ (base * m)) for i in range(count)]))
    return received


def call(body, outs, args, flops=0, in_specs=None, name=None):
    size = sum(4 * a.size for a in args) + sum(4 * o.size for o in outs)
    kwargs = {}
    if in_specs is not None:
        kwargs = {"in_specs": in_specs, "grid": (1,)}
        kwargs["out_specs"] = [whole(o.shape) for o in outs]
    return pl.pallas_call(
        body,
        out_shape=outs,
        cost_estimate=pl.CostEstimate(flops=flops, bytes_accessed=size, transcendentals=0),
        name=name,
        **kwargs,
    )(*args)


def whole(shape):
    return pl.BlockSpec(shape, lambda i: (0,) * len(shape))


def out(shape, dtype=F32):
    return jax.ShapeDtypeStruct(shape, dtype)


def put_message(ref, state, totals):
    rows, half = state.shape[0], state.shape[1] // 2
    ref[0:rows] = state[:, :half]
    ref[rows : 2 * rows] = state[:, half:]
    ref[2 * rows : 2 * rows + 8] = totals[:, :half]
    ref[2 * rows + 8 : 2 * rows + 16] = totals[:, half:]


def take_state(pieces, scratch, rows):
    mine = lax.axis_index("head")
    half = pieces[0].shape[1]
    for m, piece in enumerate(pieces):
        at = pl.ds(pl.multiple_of((mine ^ m) * rows, 8), rows)
        scratch[at, :half] = piece[0:rows]
        scratch[at, half:] = piece[rows : 2 * rows]
    totals = jnp.concatenate(
        [pieces[0][2 * rows : 2 * rows + 8], pieces[0][2 * rows + 8 : 2 * rows + 16]], axis=1
    )
    return scratch[...], totals


def key_body(share, keys, values, weight, feat_high, feat_low, message, scratch):
    mine = lax.axis_index("head")
    upper, lower = softmaxes(dot_exact(keys[...], weight[...], NN))
    feat = split(jnp.concatenate([upper, lower], axis=1))
    feat_high[...] = feat[0]
    feat_low[...] = feat[1]
    scratch[...] = dot3(split(values[...]), feat, TN)
    ones = jnp.ones((8, feat[0].shape[0]), BF16)
    totals = raw_dot(ones, feat[0], NN) + raw_dot(ones, feat[1], NN)
    state = scratch[pl.ds(pl.multiple_of(mine * share, 8), share), :]
    put_message(message, state, totals)


def causal(size):
    row = lax.broadcasted_iota(jnp.int32, (size, size), 0)
    col = lax.broadcasted_iota(jnp.int32, (size, size), 1)
    return row >= col


def query_body(
    block, queries, weight, values, key_high, key_low,
    feat_high, feat_low, score_high, score_low, numer, norm,
):
    upper, lower = softmaxes(dot_exact(queries[...], weight[0], NN))
    feat = split(jnp.concatenate([upper, lower], axis=1))
    feat_high[...] = feat[0]
    feat_low[...] = feat[1]
    rows, width = values.shape
    extended = split(jnp.concatenate([values[...], jnp.ones((rows, width), F32)], axis=1))
    mask = causal(block)
    for i in range(rows // block):
        at = slice(i * block, (i + 1) * block)
        total = None
        for j in range(i + 1):
            past = slice(j * block, (j + 1) * block)
            scores = dot3((feat[0][at], feat[1][at]), (key_high[past], key_low[past]), NT)
            if i == j:
                scores = jnp.where(mask, scores, 0.0)
            pair = split(scores)
            score_high[at, past] = pair[0]
            score_low[at, past] = pair[1]
            term = dot3(pair, (extended[0][past], extended[1][past]), NN)
            total = term if total is None else total + term
        numer[at] = total[:, :width]
        norm[at] = total[:, width:]


def scan_body(base, radix, local, *refs):
    received, (total, before) = refs[: radix - 1], refs[radix - 1 :]
    mine = (lax.axis_index("ctx") // base) % radix
    whole_sum, earlier = local[...], jnp.zeros(local.shape, F32)
    for m, piece in enumerate(received, 1):
        value = piece[...]
        whole_sum = whole_sum + value
        earlier = earlier + jnp.where((mine ^ m) < mine, value, 0.0)
    total[...] = whole_sum
    before[...] = earlier


def scan_last_body(base, radix, before, *refs):
    received, (result,) = refs[: radix - 1], refs[radix - 1 :]
    mine = (lax.axis_index("ctx") // base) % radix
    earlier = before[...]
    for m, piece in enumerate(received, 1):
        earlier = earlier + jnp.where((mine ^ m) < mine, piece[...], 0.0)
    result[...] = earlier


def inter_body(heads, peers, share, *refs):
    pieces, refs = refs[:peers], refs[peers:]
    feats, refs = [refs[2 * h : 2 * h + 2] for h in range(heads)], refs[2 * heads :]
    locals_, refs = [refs[2 * h : 2 * h + 2] for h in range(heads)], refs[2 * heads :]
    scaled, refs = refs[0], refs[1:]
    state_high, state_low = refs[:2]
    refs = refs[2:]
    grads, refs = refs[:heads], refs[heads:]
    messages, refs = refs[:peers], refs[peers:]
    scratch, = refs
    mine = lax.axis_index("head")
    state, totals = take_state(pieces, scratch, share)
    width = state.shape[0]
    reps = width // 8
    extended = split(jnp.concatenate([state] + [totals] * reps, axis=0))
    state_high[...] = extended[0]
    state_low[...] = extended[1]
    carried = None
    for h in range(heads):
        feat = (feats[h][0][...], feats[h][1][...])
        inter = dot3(feat, extended, NT)
        numer = locals_[h][0][...] + inter[:, :width]
        norm = locals_[h][1][...] + inter[:, width:]
        mine_scaled = scaled[:, h * width : (h + 1) * width]
        grad_numer = mine_scaled / norm
        along = jnp.sum(mine_scaled * (numer / norm), axis=1, keepdims=True)
        both = jnp.concatenate([grad_numer, -(along / norm)], axis=1)
        grads[h][...] = both
        term = dot3(split(both), feat, TN)
        carried = term if carried is None else carried + term
    scratch[...] = carried[:width]
    for m, message in enumerate(messages):
        part = scratch[pl.ds(pl.multiple_of((mine ^ m) * share, 8), share), :]
        put_message(message, part, carried[width : width + 8])


def query_grad_body(
    block, first, queries, weight, values, key_high, key_low, feat_high, feat_low,
    score_high, score_low, grads, state_high, state_low, *refs,
):
    earlier, (grad_input, grad_weight, grad_key) = refs[:-3], refs[-3:]
    rows, width = values.shape
    wide = key_high.shape[1]
    both = grads[...]
    numer = split(both[:, :width])
    scale = 1.0 / width
    extended = split(jnp.concatenate([both[:, :width], both[:, width:] * scale], axis=1))
    value_pair = split(values[...])
    feat = (feat_high[...], feat_low[...])
    state = (state_high[...], state_low[...])
    mask = causal(block)
    count = rows // block
    key_sums, value_sums, logit_parts = [None] * count, [None] * count, []
    cut = lambda pair, at: (pair[0][at], pair[1][at])
    for i in range(count):
        at = slice(i * block, (i + 1) * block)
        norm_part = both[at, width:]
        norm_part = jnp.concatenate([norm_part] * (block // width), axis=1)
        grad_query = dot3(cut(extended, at), state, NN)
        for j in range(i + 1):
            past = slice(j * block, (j + 1) * block)
            grad_scores = dot3(cut(numer, at), cut(value_pair, past), NT) + norm_part
            if i == j:
                grad_scores = jnp.where(mask, grad_scores, 0.0)
            pair = split(grad_scores)
            keys = (key_high[past], key_low[past])
            grad_query = grad_query + dot3(pair, keys, NN)
            key_term = dot3(pair, cut(feat, at), TN)
            value_term = dot3((score_high[at, past], score_low[at, past]), cut(numer, at), TN)
            key_sums[j] = key_term if key_sums[j] is None else key_sums[j] + key_term
            value_sums[j] = value_term if value_sums[j] is None else value_sums[j] + value_term
        logit_parts.append(logit_grad(joined(cut(feat, at)), grad_query))
    grad_logits = split(jnp.concatenate(logit_parts, axis=0))
    grad_input[...] = dot3(grad_logits, split(weight[0]), NT)
    grad_weight[...] = dot3(split(queries[...]), grad_logits, TN)
    for j in range(count):
        past = slice(j * block, (j + 1) * block)
        if first:
            grad_key[past, :wide] = key_sums[j]
            grad_key[past, wide:] = value_sums[j]
        else:
            grad_key[past, :wide] = earlier[0][past, :wide] + key_sums[j]
            grad_key[past, wide:] = earlier[0][past, wide:] + value_sums[j]


def part_body(part, *refs):
    source, targets = refs[0], refs[1:]
    mine = lax.axis_index("head")
    for m, target in enumerate(targets):
        target[...] = source[pl.ds(pl.multiple_of((mine ^ m) * part, 8), part), :]


def sum_body(*refs):
    total = refs[0][...]
    for piece in refs[1:-1]:
        total = total + piece[...]
    refs[-1][...] = total


def suffix_body(base, radix, above, local, *refs):
    received, (later, *messages) = refs[: above - 1], refs[above - 1 :]
    mine = (lax.axis_index("ctx") // base) % radix
    upper = (lax.axis_index("ctx") // (base * radix)) % above
    total = jnp.zeros(local.shape, F32)
    for m, piece in enumerate(received, 1):
        total = total + jnp.where((upper ^ m) > upper, piece[...], 0.0)
    later[...] = total
    for m, message in enumerate(messages, 1):
        message[...] = total + jnp.where(mine > (mine ^ m), local[...], 0.0)


def suffix_weight_body(base, radix, above, heads, local, *refs):
    received, refs = refs[: above - 1], refs[above - 1 :]
    weights, (later, kept, *messages) = refs[:heads], refs[heads:]
    scratch = messages.pop()
    mine = (lax.axis_index("ctx") // base) % radix
    upper = (lax.axis_index("ctx") // (base * radix)) % above
    size = local.shape[0]
    width = weights[0].shape[0]
    shard = heads * width // radix
    for h, weight in enumerate(weights):
        scratch[h * width : (h + 1) * width] = weight[...]
    total = jnp.zeros(local.shape, F32)
    for m, piece in enumerate(received, 1):
        total = total + jnp.where((upper ^ m) > upper, piece[...], 0.0)
    later[...] = total
    rows = lambda m: pl.ds(pl.multiple_of((mine ^ m) * shard, 8), shard)
    kept[...] = scratch[rows(0), :]
    for m, message in enumerate(messages, 1):
        message[0:size] = total + jnp.where(mine > (mine ^ m), local[...], 0.0)
        message[size : size + shard] = scratch[rows(m), :]


def suffix_last_body(later, kept, *refs):
    received, (result, shard) = refs[:-2], refs[-2:]
    size = later.shape[0]
    total, sums = later[...], kept[...]
    for piece in received:
        total = total + piece[0:size]
        sums = sums + piece[size : size + sums.shape[0]]
    result[...] = total
    shard[...] = sums


def key_grad_body(peers, share, part, *refs):
    pieces, refs = refs[:peers], refs[peers:]
    inner, refs = refs[:peers], refs[peers:]
    values, keys, key_high, key_low = refs[:4]
    logit_ref, value_ref, state_high, state_low, *parts = refs[4:]
    scratch, weights = parts.pop(-2), parts.pop(-1)
    mine = lax.axis_index("head")
    state, totals = take_state(pieces, scratch, share)
    state = split(state)
    state_high[...] = state[0]
    state_low[...] = state[1]
    at = pl.ds(pl.multiple_of(mine * part, 8), part)
    feat = (key_high[at, :], key_low[at, :])
    wide = feat[0].shape[1]
    grad = dot3(split(values[at, :]), state, NN) + totals[0:1]
    value = inner[0][:, wide:]
    for piece in inner:
        grad = grad + piece[:, :wide]
    for piece in inner[1:]:
        value = value + piece[:, wide:]
    value_ref[...] = value
    grad_logits = logit_grad(joined(feat), grad)
    logit_ref[...] = grad_logits
    weights[...] = dot3(split(keys[at, :]), split(grad_logits), TN)
    rows = parts[0].shape[0]
    for m, target in enumerate(parts):
        target[...] = weights[pl.ds(pl.multiple_of((mine ^ m) * rows, 8), rows), :]


def key_out_body(part, logits, values, state_high, state_low, weight, key_high, key_low, grad_key, grad_value):
    at = pl.ds(pl.multiple_of(lax.axis_index("head") * part, 8), part)
    grad_key[...] = dot3(split(logits[...]), split(weight[...]), NT)
    feat = (key_high[at, :], key_low[at, :])
    grad_value[...] = values[...] + dot3(feat, (state_high[...], state_low[...]), NT)


def weight_message_body(*refs):
    parts, shard, message = refs[:-2], refs[-2], refs[-1]
    total = parts[0][...]
    for piece in parts[1:]:
        total = total + piece[...]
    rows = total.shape[0]
    message[0:rows] = total
    message[rows:] = shard[...]


def weight_last_body(base, radix, rows, local, *refs):
    received, (share, gathered) = refs[: radix - 1], refs[radix - 1 :]
    mine = (lax.axis_index("ctx") // base) % radix
    total = local[0:rows]
    shard = local.shape[0] - rows
    gathered[pl.ds(pl.multiple_of(mine * shard, 8), shard), :] = local[rows:]
    for m, piece in enumerate(received, 1):
        total = total + piece[0:rows]
        at = pl.ds(pl.multiple_of((mine ^ m) * shard, 8), shard)
        gathered[at, :] = piece[rows:]
    share[...] = total


def gather_body(rows, *refs):
    pieces, result = refs[:-1], refs[-1]
    mine = lax.axis_index("head")
    for m, piece in enumerate(pieces):
        result[pl.ds(pl.multiple_of((mine ^ m) * rows, 8), rows), :] = piece[...]


def with_scratch(body, outs, args, scratch, flops=0, name=None):
    size = sum(4 * a.size for a in args) + sum(4 * o.size for o in outs)
    return pl.pallas_call(
        body,
        out_shape=outs,
        scratch_shapes=scratch,
        cost_estimate=pl.CostEstimate(flops=flops, bytes_accessed=size, transcendentals=0),
        name=name,
    )(*args)


def on_device(queries, keys, values, cotangent, source_ids, source_weights, q_feature, k_feature):
    heads, width, half = q_feature.shape
    wide = 2 * half
    rows = queries.shape[0]
    peers = lax.axis_size("head")
    share = width // peers
    part = rows // peers
    block = min(256, rows)
    digits = digits_of(lax.axis_size("ctx"))
    message = (2 * share + 16, half)
    bind = functools.partial
    unit = 2 * rows * width * wide

    source_index = lax.broadcasted_iota(jnp.int32, (1, source_weights.shape[0]), 1)
    lookup = source_ids[:, None] == source_index
    weight = jnp.sum(jnp.where(lookup, source_weights[None, :], 0.0), axis=1)
    scaled = cotangent * weight[:, None]

    feat_shape = out((rows, wide), BF16)
    key_high, key_low, local = with_scratch(
        bind(key_body, share),
        [feat_shape, feat_shape, out(message)],
        (keys, values, k_feature),
        [pltpu.VMEM((width, wide), F32)],
        6 * unit,
        "key_features",
    )

    before, total = None, local
    for place, (base, radix) in enumerate(digits):
        received = exchange(total, "ctx", base, radix)
        if place == 0:
            total, before = call(
                bind(scan_body, base, radix), [out(message)] * 2, (total, *received), name="scan"
            )
        else:
            more = before
            (before,) = call(
                bind(scan_last_body, base, radix), [out(message)], (more, *received), name="scan_last"
            )
            if place + 1 < len(digits):
                total = sum(received, total)
    prefix = [before] + exchange(before, "head", 1, peers)

    feats, scores, inner = [], [], []
    for h in range(heads):
        results = call(
            bind(query_body, block),
            [feat_shape] * 2 + [out((rows, rows), BF16)] * 2 + [out((rows, width))] * 2,
            (queries, q_feature, values, key_high, key_low),
            9 * unit,
            [
                pl.BlockSpec((rows, width), lambda i, h=h: (0, h)),
                pl.BlockSpec((1, width, half), lambda i, h=h: (h, 0, 0)),
                whole((rows, width)),
                whole((rows, wide)),
                whole((rows, wide)),
            ],
            "query_features",
        )
        feats.append(results[0:2])
        scores.append(results[2:4])
        inner.append(results[4:6])

    results = with_scratch(
        bind(inter_body, heads, peers, share),
        [out((2 * width, wide), BF16)] * 2
        + [out((rows, 2 * width))] * heads
        + [out(message)] * peers,
        (
            *prefix,
            *[x for pair in feats for x in pair],
            *[x for pair in inner for x in pair],
            scaled,
        ),
        [pltpu.VMEM((width, wide), F32)],
        12 * heads * unit,
        "inter",
    )
    state, results = results[:2], results[2:]
    grads, results = results[:heads], results[heads:]
    sends = exchange(results[1:], "head", 1, peers)
    (carried,) = call(sum_body, [out(message)], (results[0], *sends), name="carried_sum")

    query_grads, weight_grads, key_inner = [], [], None
    for h in range(heads):
        args = [
            queries, q_feature, values, key_high, key_low, *feats[h], *scores[h], grads[h], *state,
        ]
        specs = [
            pl.BlockSpec((rows, width), lambda i, h=h: (0, h)),
            pl.BlockSpec((1, width, half), lambda i, h=h: (h, 0, 0)),
        ] + [whole(a.shape) for a in args[2:]]
        if h > 0:
            args.append(key_inner)
            specs.append(whole(key_inner.shape))
        grad_input, grad_weight, key_inner = call(
            bind(query_grad_body, block, h == 0),
            [out((rows, width)), out((width, half)), out((rows, wide + width))],
            args,
            15 * unit,
            specs,
            "query_grads",
        )
        query_grads.append(grad_input)
        weight_grads.append(grad_weight)
    parts = call(
        bind(part_body, part), [out((part, wide + width))] * peers, (key_inner,), name="parts"
    )
    inner_parts = [parts[0]] + exchange(parts[1:], "head", 1, peers)

    later, messages = None, carried
    base_low, radix_low = digits[0]
    shard = heads * width // radix_low
    for place in range(len(digits) - 1, 0, -1):
        base, radix = digits[place]
        received = exchange(messages, "ctx", base, radix)
        below_base, below_radix = digits[place - 1]
        if place == 1 and len(digits) == 2:
            results = with_scratch(
                bind(suffix_weight_body, base_low, radix_low, radix, heads),
                [out(message), out((shard, half))]
                + [out((message[0] + shard, half))] * (radix_low - 1),
                (carried, *received, *weight_grads),
                [pltpu.VMEM((heads * width, half), F32)],
                name="suffix_weight",
            )
            later, kept, messages = results[0], results[1], results[2:]
        else:
            mine = (lax.axis_index("ctx") // base) % radix
            if place == len(digits) - 1:
                later = sum(jnp.where((mine ^ m) > mine, r, 0.0) for m, r in enumerate(received, 1))
            else:
                later = sum(received, later)
            below = (lax.axis_index("ctx") // below_base) % below_radix
            messages = [
                later + jnp.where(below > (below ^ m), carried, 0.0) for m in range(1, below_radix)
            ]
            if place == 1:
                stacked = jnp.concatenate(weight_grads, axis=0)
                cut = lambda m: lax.dynamic_slice_in_dim(stacked, (below ^ m) * shard, shard, 0)
                kept = cut(0)
                messages = [
                    jnp.concatenate([part_message, cut(m)], axis=0)
                    for m, part_message in enumerate(messages, 1)
                ]
    received = exchange(messages, "ctx", base_low, radix_low)
    later, q_shard = call(
        suffix_last_body,
        [out(message), out((shard, half))],
        (later, kept, *received),
        name="suffix_last",
    )
    suffix = [later] + exchange(later, "head", 1, peers)

    weight_rows = width // peers
    results = with_scratch(
        bind(key_grad_body, peers, share, part),
        [out((part, half)), out((part, width))]
        + [out((width, wide), BF16)] * 2
        + [out((weight_rows, half))] * peers,
        (*suffix, *inner_parts, values, keys, key_high, key_low),
        [pltpu.VMEM((width, wide), F32), pltpu.VMEM((width, half), F32)],
        3 * unit,
        "key_grads",
    )
    key_logits, value_inner, later_high, later_low = results[:4]
    weight_parts = results[4:]
    weight_parts = [weight_parts[0]] + exchange(weight_parts[1:], "head", 1, peers)
    (total,) = call(
        weight_message_body,
        [out((weight_rows + shard, half))],
        (*weight_parts, q_shard),
        name="weight_message",
    )
    for base, radix in digits[:0:-1]:
        received = exchange(total, "ctx", base, radix)
        (total,) = call(sum_body, [out(total.shape)], (total, *received), name="weight_sum")
    received = exchange(total, "ctx", base_low, radix_low)
    k_share, q_sum = call(
        bind(weight_last_body, base_low, radix_low, weight_rows),
        [out((weight_rows, half)), out((heads * width, half))],
        (total, *received),
        name="weight_last",
    )
    shares = [k_share] + exchange(k_share, "head", 1, peers)
    (k_sum,) = call(bind(gather_body, weight_rows), [out((width, half))], shares, name="gather")

    grad_keys, grad_values = call(
        bind(key_out_body, part),
        [out((part, width))] * 2,
        (key_logits, value_inner, later_high, later_low, k_feature, key_high, key_low),
        3 * unit,
        name="key_out",
    )
    return (
        jnp.concatenate(query_grads, axis=1),
        grad_keys,
        grad_values,
        q_sum.reshape(heads, width, half),
        k_sum,
    )


def solution(mesh):
    placed = (
        P("ctx", "head"),
        P("ctx", None),
        P("ctx", None),
        P("ctx", "head"),
        P("ctx"),
        P(),
        P("head", None, None),
        P(),
    )
    return jax.shard_map(
        on_device,
        mesh=mesh,
        in_specs=placed,
        out_specs=(
            P("ctx", "head"),
            P(("ctx", "head"), None),
            P(("ctx", "head"), None),
            P("head", None, None),
            P(),
        ),
        check_vma=False,
    )
```

```python
import functools

import jax
import jax.numpy as jnp
from jax import lax
from jax.experimental import pallas as pl
from jax.experimental.pallas import tpu as pltpu
from jax.sharding import PartitionSpec as P


F32 = jnp.float32
BF16 = jnp.bfloat16
NN = ((1,), (0,))
NT = ((1,), (1,))
TN = ((0,), (0,))


def split(x):
    high = x.astype(BF16)
    return high, (x - high.astype(F32)).astype(BF16)


def joined(pair):
    return pair[0].astype(F32) + pair[1].astype(F32)


def raw_dot(a, b, dims):
    return lax.dot_general(a, b, (dims, ((), ())), preferred_element_type=F32)


def dot3(a, b, dims):
    return raw_dot(a[0], b[0], dims) + (raw_dot(a[0], b[1], dims) + raw_dot(a[1], b[0], dims))


def dot_exact(a, b, dims):
    return lax.dot_general(
        a, b, (dims, ((), ())), precision=lax.Precision.HIGHEST, preferred_element_type=F32
    )


def softmaxes(logits):
    upper = jnp.exp(logits - jnp.max(logits, axis=-1, keepdims=True))
    lower = jnp.exp(jnp.min(logits, axis=-1, keepdims=True) - logits)
    return (
        upper / jnp.sum(upper, axis=-1, keepdims=True),
        lower / jnp.sum(lower, axis=-1, keepdims=True),
    )


def logit_grad(features, grad):
    half = features.shape[1] // 2
    upper, lower = features[:, :half], features[:, half:]
    a, b = grad[:, :half], grad[:, half:]
    up = upper * (a - jnp.sum(upper * a, axis=-1, keepdims=True))
    return up - lower * (b - jnp.sum(lower * b, axis=-1, keepdims=True))


def digits_of(count):
    found, base = [], 1
    while base < count:
        radix = 4 if (count // base) % 4 == 0 else 2
        found.append((base, radix))
        base *= radix
    return found


def exchange(values, axis, base, radix):
    count = lax.axis_size(axis)
    received = []
    for m in range(1, radix):
        value = values[m - 1] if isinstance(values, (list, tuple)) else values
        received.append(lax.ppermute(value, axis, [(i, i ^ (base * m)) for i in range(count)]))
    return received


def grant(size):
    return (4 << 20) + 3 * size


def call(body, outs, args, flops=0, in_specs=None, name=None):
    size = sum(4 * a.size for a in args) + sum(4 * o.size for o in outs)
    kwargs = {}
    if in_specs is not None:
        kwargs = {"in_specs": in_specs, "grid": (1,)}
        kwargs["out_specs"] = [whole(o.shape) for o in outs]
    return pl.pallas_call(
        body,
        out_shape=outs,
        cost_estimate=pl.CostEstimate(flops=flops, bytes_accessed=size, transcendentals=0),
        compiler_params=pltpu.CompilerParams(vmem_limit_bytes=grant(size)),
        name=name,
        **kwargs,
    )(*args)


def whole(shape):
    return pl.BlockSpec(shape, lambda i: (0,) * len(shape))


def out(shape, dtype=F32):
    return jax.ShapeDtypeStruct(shape, dtype)


def put_message(ref, state, totals):
    rows, half = state.shape[0], state.shape[1] // 2
    ref[0:rows] = state[:, :half]
    ref[rows : 2 * rows] = state[:, half:]
    ref[2 * rows : 2 * rows + 8] = totals[:, :half]
    ref[2 * rows + 8 : 2 * rows + 16] = totals[:, half:]


def take_state(pieces, scratch, rows):
    mine = lax.axis_index("head")
    half = pieces[0].shape[1]
    for m, piece in enumerate(pieces):
        at = pl.ds(pl.multiple_of((mine ^ m) * rows, 8), rows)
        scratch[at, :half] = piece[0:rows]
        scratch[at, half:] = piece[rows : 2 * rows]
    totals = jnp.concatenate(
        [pieces[0][2 * rows : 2 * rows + 8], pieces[0][2 * rows + 8 : 2 * rows + 16]], axis=1
    )
    return scratch[...], totals


def key_body(share, keys, values, weight, feat_high, feat_low, message, scratch):
    mine = lax.axis_index("head")
    upper, lower = softmaxes(dot_exact(keys[...], weight[...], NN))
    feat = split(jnp.concatenate([upper, lower], axis=1))
    feat_high[...] = feat[0]
    feat_low[...] = feat[1]
    scratch[...] = dot3(split(values[...]), feat, TN)
    ones = jnp.ones((8, feat[0].shape[0]), BF16)
    totals = raw_dot(ones, feat[0], NN) + raw_dot(ones, feat[1], NN)
    state = scratch[pl.ds(pl.multiple_of(mine * share, 8), share), :]
    put_message(message, state, totals)


def causal(size):
    row = lax.broadcasted_iota(jnp.int32, (size, size), 0)
    col = lax.broadcasted_iota(jnp.int32, (size, size), 1)
    return row >= col


def query_body(
    block, queries, weight, values, key_high, key_low,
    feat_high, feat_low, score_high, score_low, numer, norm,
):
    upper, lower = softmaxes(dot_exact(queries[...], weight[0], NN))
    feat = split(jnp.concatenate([upper, lower], axis=1))
    feat_high[...] = feat[0]
    feat_low[...] = feat[1]
    rows, width = values.shape
    extended = split(jnp.concatenate([values[...], jnp.ones((rows, width), F32)], axis=1))
    mask = causal(block)
    for i in range(rows // block):
        at = slice(i * block, (i + 1) * block)
        total = None
        for j in range(i + 1):
            past = slice(j * block, (j + 1) * block)
            scores = dot3((feat[0][at], feat[1][at]), (key_high[past], key_low[past]), NT)
            if i == j:
                scores = jnp.where(mask, scores, 0.0)
            pair = split(scores)
            score_high[at, past] = pair[0]
            score_low[at, past] = pair[1]
            term = dot3(pair, (extended[0][past], extended[1][past]), NN)
            total = term if total is None else total + term
        numer[at] = total[:, :width]
        norm[at] = total[:, width:]


def scan_body(base, radix, local, *refs):
    received, (total, before) = refs[: radix - 1], refs[radix - 1 :]
    mine = (lax.axis_index("ctx") // base) % radix
    whole_sum, earlier = local[...], jnp.zeros(local.shape, F32)
    for m, piece in enumerate(received, 1):
        value = piece[...]
        whole_sum = whole_sum + value
        earlier = earlier + jnp.where((mine ^ m) < mine, value, 0.0)
    total[...] = whole_sum
    before[...] = earlier


def scan_last_body(base, radix, before, *refs):
    received, (result,) = refs[: radix - 1], refs[radix - 1 :]
    mine = (lax.axis_index("ctx") // base) % radix
    earlier = before[...]
    for m, piece in enumerate(received, 1):
        earlier = earlier + jnp.where((mine ^ m) < mine, piece[...], 0.0)
    result[...] = earlier


def inter_body(heads, peers, share, *refs):
    pieces, refs = refs[:peers], refs[peers:]
    feats, refs = [refs[2 * h : 2 * h + 2] for h in range(heads)], refs[2 * heads :]
    locals_, refs = [refs[2 * h : 2 * h + 2] for h in range(heads)], refs[2 * heads :]
    scaled, refs = refs[0], refs[1:]
    state_high, state_low = refs[:2]
    refs = refs[2:]
    grads, refs = refs[:heads], refs[heads:]
    messages, refs = refs[:peers], refs[peers:]
    scratch, = refs
    mine = lax.axis_index("head")
    state, totals = take_state(pieces, scratch, share)
    width = state.shape[0]
    reps = width // 8
    extended = split(jnp.concatenate([state] + [totals] * reps, axis=0))
    state_high[...] = extended[0]
    state_low[...] = extended[1]
    carried = None
    for h in range(heads):
        feat = (feats[h][0][...], feats[h][1][...])
        inter = dot3(feat, extended, NT)
        numer = locals_[h][0][...] + inter[:, :width]
        norm = locals_[h][1][...] + inter[:, width:]
        mine_scaled = scaled[:, h * width : (h + 1) * width]
        grad_numer = mine_scaled / norm
        along = jnp.sum(mine_scaled * (numer / norm), axis=1, keepdims=True)
        both = jnp.concatenate([grad_numer, -(along / norm)], axis=1)
        grads[h][...] = both
        term = dot3(split(both), feat, TN)
        carried = term if carried is None else carried + term
    scratch[...] = carried[:width]
    for m, message in enumerate(messages):
        part = scratch[pl.ds(pl.multiple_of((mine ^ m) * share, 8), share), :]
        put_message(message, part, carried[width : width + 8])


def query_grad_body(
    block, first, queries, weight, values, key_high, key_low, feat_high, feat_low,
    score_high, score_low, grads, state_high, state_low, *refs,
):
    earlier, (grad_input, grad_weight, grad_key) = refs[:-3], refs[-3:]
    rows, width = values.shape
    wide = key_high.shape[1]
    both = grads[...]
    numer = split(both[:, :width])
    scale = 1.0 / width
    extended = split(jnp.concatenate([both[:, :width], both[:, width:] * scale], axis=1))
    value_pair = split(values[...])
    feat = (feat_high[...], feat_low[...])
    state = (state_high[...], state_low[...])
    mask = causal(block)
    count = rows // block
    key_sums, value_sums, logit_parts = [None] * count, [None] * count, []
    cut = lambda pair, at: (pair[0][at], pair[1][at])
    for i in range(count):
        at = slice(i * block, (i + 1) * block)
        norm_part = both[at, width:]
        norm_part = jnp.concatenate([norm_part] * (block // width), axis=1)
        grad_query = dot3(cut(extended, at), state, NN)
        for j in range(i + 1):
            past = slice(j * block, (j + 1) * block)
            grad_scores = dot3(cut(numer, at), cut(value_pair, past), NT) + norm_part
            if i == j:
                grad_scores = jnp.where(mask, grad_scores, 0.0)
            pair = split(grad_scores)
            keys = (key_high[past], key_low[past])
            grad_query = grad_query + dot3(pair, keys, NN)
            key_term = dot3(pair, cut(feat, at), TN)
            value_term = dot3((score_high[at, past], score_low[at, past]), cut(numer, at), TN)
            key_sums[j] = key_term if key_sums[j] is None else key_sums[j] + key_term
            value_sums[j] = value_term if value_sums[j] is None else value_sums[j] + value_term
        logit_parts.append(logit_grad(joined(cut(feat, at)), grad_query))
    grad_logits = split(jnp.concatenate(logit_parts, axis=0))
    grad_input[...] = dot3(grad_logits, split(weight[0]), NT)
    grad_weight[...] = dot3(split(queries[...]), grad_logits, TN)
    for j in range(count):
        past = slice(j * block, (j + 1) * block)
        if first:
            grad_key[past, :wide] = key_sums[j]
            grad_key[past, wide:] = value_sums[j]
        else:
            grad_key[past, :wide] = earlier[0][past, :wide] + key_sums[j]
            grad_key[past, wide:] = earlier[0][past, wide:] + value_sums[j]


def part_body(part, *refs):
    source, targets = refs[0], refs[1:]
    mine = lax.axis_index("head")
    for m, target in enumerate(targets):
        target[...] = source[pl.ds(pl.multiple_of((mine ^ m) * part, 8), part), :]


def sum_body(*refs):
    total = refs[0][...]
    for piece in refs[1:-1]:
        total = total + piece[...]
    refs[-1][...] = total


def suffix_body(base, radix, above, local, *refs):
    received, (later, *messages) = refs[: above - 1], refs[above - 1 :]
    mine = (lax.axis_index("ctx") // base) % radix
    upper = (lax.axis_index("ctx") // (base * radix)) % above
    total = jnp.zeros(local.shape, F32)
    for m, piece in enumerate(received, 1):
        total = total + jnp.where((upper ^ m) > upper, piece[...], 0.0)
    later[...] = total
    for m, message in enumerate(messages, 1):
        message[...] = total + jnp.where(mine > (mine ^ m), local[...], 0.0)


def suffix_weight_body(base, radix, above, heads, local, *refs):
    received, refs = refs[: above - 1], refs[above - 1 :]
    weights, (later, kept, *messages) = refs[:heads], refs[heads:]
    scratch = messages.pop()
    mine = (lax.axis_index("ctx") // base) % radix
    upper = (lax.axis_index("ctx") // (base * radix)) % above
    size = local.shape[0]
    width = weights[0].shape[0]
    shard = heads * width // radix
    for h, weight in enumerate(weights):
        scratch[h * width : (h + 1) * width] = weight[...]
    total = jnp.zeros(local.shape, F32)
    for m, piece in enumerate(received, 1):
        total = total + jnp.where((upper ^ m) > upper, piece[...], 0.0)
    later[...] = total
    rows = lambda m: pl.ds(pl.multiple_of((mine ^ m) * shard, 8), shard)
    kept[...] = scratch[rows(0), :]
    for m, message in enumerate(messages, 1):
        message[0:size] = total + jnp.where(mine > (mine ^ m), local[...], 0.0)
        message[size : size + shard] = scratch[rows(m), :]


def suffix_last_body(later, kept, *refs):
    received, (result, shard) = refs[:-2], refs[-2:]
    size = later.shape[0]
    total, sums = later[...], kept[...]
    for piece in received:
        total = total + piece[0:size]
        sums = sums + piece[size : size + sums.shape[0]]
    result[...] = total
    shard[...] = sums


def key_grad_body(peers, share, part, *refs):
    pieces, refs = refs[:peers], refs[peers:]
    inner, refs = refs[:peers], refs[peers:]
    values, keys, key_high, key_low = refs[:4]
    logit_ref, value_ref, state_high, state_low, *parts = refs[4:]
    scratch, weights = parts.pop(-2), parts.pop(-1)
    mine = lax.axis_index("head")
    state, totals = take_state(pieces, scratch, share)
    state = split(state)
    state_high[...] = state[0]
    state_low[...] = state[1]
    at = pl.ds(pl.multiple_of(mine * part, 8), part)
    feat = (key_high[at, :], key_low[at, :])
    wide = feat[0].shape[1]
    grad = dot3(split(values[at, :]), state, NN) + totals[0:1]
    value = inner[0][:, wide:]
    for piece in inner:
        grad = grad + piece[:, :wide]
    for piece in inner[1:]:
        value = value + piece[:, wide:]
    value_ref[...] = value
    grad_logits = logit_grad(joined(feat), grad)
    logit_ref[...] = grad_logits
    weights[...] = dot3(split(keys[at, :]), split(grad_logits), TN)
    rows = parts[0].shape[0]
    for m, target in enumerate(parts):
        target[...] = weights[pl.ds(pl.multiple_of((mine ^ m) * rows, 8), rows), :]


def key_out_body(part, logits, values, state_high, state_low, weight, key_high, key_low, grad_key, grad_value):
    at = pl.ds(pl.multiple_of(lax.axis_index("head") * part, 8), part)
    grad_key[...] = dot3(split(logits[...]), split(weight[...]), NT)
    feat = (key_high[at, :], key_low[at, :])
    grad_value[...] = values[...] + dot3(feat, (state_high[...], state_low[...]), NT)


def weight_message_body(*refs):
    parts, shard, message = refs[:-2], refs[-2], refs[-1]
    total = parts[0][...]
    for piece in parts[1:]:
        total = total + piece[...]
    rows = total.shape[0]
    message[0:rows] = total
    message[rows:] = shard[...]


def weight_last_body(base, radix, rows, local, *refs):
    received, (share, gathered) = refs[: radix - 1], refs[radix - 1 :]
    mine = (lax.axis_index("ctx") // base) % radix
    total = local[0:rows]
    shard = local.shape[0] - rows
    gathered[pl.ds(pl.multiple_of(mine * shard, 8), shard), :] = local[rows:]
    for m, piece in enumerate(received, 1):
        total = total + piece[0:rows]
        at = pl.ds(pl.multiple_of((mine ^ m) * shard, 8), shard)
        gathered[at, :] = piece[rows:]
    share[...] = total


def gather_body(rows, *refs):
    pieces, result = refs[:-1], refs[-1]
    mine = lax.axis_index("head")
    for m, piece in enumerate(pieces):
        result[pl.ds(pl.multiple_of((mine ^ m) * rows, 8), rows), :] = piece[...]


def with_scratch(body, outs, args, scratch, flops=0, name=None):
    size = sum(4 * a.size for a in args) + sum(4 * o.size for o in outs)
    return pl.pallas_call(
        body,
        out_shape=outs,
        scratch_shapes=scratch,
        cost_estimate=pl.CostEstimate(flops=flops, bytes_accessed=size, transcendentals=0),
        compiler_params=pltpu.CompilerParams(vmem_limit_bytes=grant(size)),
        name=name,
    )(*args)


def on_device(queries, keys, values, cotangent, source_ids, source_weights, q_feature, k_feature):
    heads, width, half = q_feature.shape
    wide = 2 * half
    rows = queries.shape[0]
    peers = lax.axis_size("head")
    share = width // peers
    part = rows // peers
    block = min(256, rows)
    digits = digits_of(lax.axis_size("ctx"))
    message = (2 * share + 16, half)
    bind = functools.partial
    unit = 2 * rows * width * wide

    source_index = lax.broadcasted_iota(jnp.int32, (1, source_weights.shape[0]), 1)
    lookup = source_ids[:, None] == source_index
    weight = jnp.sum(jnp.where(lookup, source_weights[None, :], 0.0), axis=1)
    scaled = cotangent * weight[:, None]

    feat_shape = out((rows, wide), BF16)
    key_high, key_low, local = with_scratch(
        bind(key_body, share),
        [feat_shape, feat_shape, out(message)],
        (keys, values, k_feature),
        [pltpu.VMEM((width, wide), F32)],
        6 * unit,
        "key_features",
    )

    before, total = None, local
    for place, (base, radix) in enumerate(digits):
        received = exchange(total, "ctx", base, radix)
        if place == 0:
            total, before = call(
                bind(scan_body, base, radix), [out(message)] * 2, (total, *received), name="scan"
            )
        else:
            more = before
            (before,) = call(
                bind(scan_last_body, base, radix), [out(message)], (more, *received), name="scan_last"
            )
            if place + 1 < len(digits):
                total = sum(received, total)
    prefix = [before] + exchange(before, "head", 1, peers)

    feats, scores, inner = [], [], []
    for h in range(heads):
        results = call(
            bind(query_body, block),
            [feat_shape] * 2 + [out((rows, rows), BF16)] * 2 + [out((rows, width))] * 2,
            (queries, q_feature, values, key_high, key_low),
            9 * unit,
            [
                pl.BlockSpec((rows, width), lambda i, h=h: (0, h)),
                pl.BlockSpec((1, width, half), lambda i, h=h: (h, 0, 0)),
                whole((rows, width)),
                whole((rows, wide)),
                whole((rows, wide)),
            ],
            "query_features",
        )
        feats.append(results[0:2])
        scores.append(results[2:4])
        inner.append(results[4:6])

    results = with_scratch(
        bind(inter_body, heads, peers, share),
        [out((2 * width, wide), BF16)] * 2
        + [out((rows, 2 * width))] * heads
        + [out(message)] * peers,
        (
            *prefix,
            *[x for pair in feats for x in pair],
            *[x for pair in inner for x in pair],
            scaled,
        ),
        [pltpu.VMEM((width, wide), F32)],
        12 * heads * unit,
        "inter",
    )
    state, results = results[:2], results[2:]
    grads, results = results[:heads], results[heads:]
    sends = exchange(results[1:], "head", 1, peers)
    (carried,) = call(sum_body, [out(message)], (results[0], *sends), name="carried_sum")

    query_grads, weight_grads, key_inner = [], [], None
    for h in range(heads):
        args = [
            queries, q_feature, values, key_high, key_low, *feats[h], *scores[h], grads[h], *state,
        ]
        specs = [
            pl.BlockSpec((rows, width), lambda i, h=h: (0, h)),
            pl.BlockSpec((1, width, half), lambda i, h=h: (h, 0, 0)),
        ] + [whole(a.shape) for a in args[2:]]
        if h > 0:
            args.append(key_inner)
            specs.append(whole(key_inner.shape))
        grad_input, grad_weight, key_inner = call(
            bind(query_grad_body, block, h == 0),
            [out((rows, width)), out((width, half)), out((rows, wide + width))],
            args,
            15 * unit,
            specs,
            "query_grads",
        )
        query_grads.append(grad_input)
        weight_grads.append(grad_weight)
    parts = call(
        bind(part_body, part), [out((part, wide + width))] * peers, (key_inner,), name="parts"
    )
    inner_parts = [parts[0]] + exchange(parts[1:], "head", 1, peers)

    later, messages = None, carried
    base_low, radix_low = digits[0]
    shard = heads * width // radix_low
    for place in range(len(digits) - 1, 0, -1):
        base, radix = digits[place]
        received = exchange(messages, "ctx", base, radix)
        below_base, below_radix = digits[place - 1]
        if place == 1 and len(digits) == 2:
            results = with_scratch(
                bind(suffix_weight_body, base_low, radix_low, radix, heads),
                [out(message), out((shard, half))]
                + [out((message[0] + shard, half))] * (radix_low - 1),
                (carried, *received, *weight_grads),
                [pltpu.VMEM((heads * width, half), F32)],
                name="suffix_weight",
            )
            later, kept, messages = results[0], results[1], results[2:]
        else:
            mine = (lax.axis_index("ctx") // base) % radix
            if place == len(digits) - 1:
                later = sum(jnp.where((mine ^ m) > mine, r, 0.0) for m, r in enumerate(received, 1))
            else:
                later = sum(received, later)
            below = (lax.axis_index("ctx") // below_base) % below_radix
            messages = [
                later + jnp.where(below > (below ^ m), carried, 0.0) for m in range(1, below_radix)
            ]
            if place == 1:
                stacked = jnp.concatenate(weight_grads, axis=0)
                cut = lambda m: lax.dynamic_slice_in_dim(stacked, (below ^ m) * shard, shard, 0)
                kept = cut(0)
                messages = [
                    jnp.concatenate([part_message, cut(m)], axis=0)
                    for m, part_message in enumerate(messages, 1)
                ]
    received = exchange(messages, "ctx", base_low, radix_low)
    later, q_shard = call(
        suffix_last_body,
        [out(message), out((shard, half))],
        (later, kept, *received),
        name="suffix_last",
    )
    suffix = [later] + exchange(later, "head", 1, peers)

    weight_rows = width // peers
    results = with_scratch(
        bind(key_grad_body, peers, share, part),
        [out((part, half)), out((part, width))]
        + [out((width, wide), BF16)] * 2
        + [out((weight_rows, half))] * peers,
        (*suffix, *inner_parts, values, keys, key_high, key_low),
        [pltpu.VMEM((width, wide), F32), pltpu.VMEM((width, half), F32)],
        3 * unit,
        "key_grads",
    )
    key_logits, value_inner, later_high, later_low = results[:4]
    weight_parts = results[4:]
    weight_parts = [weight_parts[0]] + exchange(weight_parts[1:], "head", 1, peers)
    (total,) = call(
        weight_message_body,
        [out((weight_rows + shard, half))],
        (*weight_parts, q_shard),
        name="weight_message",
    )
    for base, radix in digits[:0:-1]:
        received = exchange(total, "ctx", base, radix)
        (total,) = call(sum_body, [out(total.shape)], (total, *received), name="weight_sum")
    received = exchange(total, "ctx", base_low, radix_low)
    k_share, q_sum = call(
        bind(weight_last_body, base_low, radix_low, weight_rows),
        [out((weight_rows, half)), out((heads * width, half))],
        (total, *received),
        name="weight_last",
    )
    shares = [k_share] + exchange(k_share, "head", 1, peers)
    (k_sum,) = call(bind(gather_body, weight_rows), [out((width, half))], shares, name="gather")

    grad_keys, grad_values = call(
        bind(key_out_body, part),
        [out((part, width))] * 2,
        (key_logits, value_inner, later_high, later_low, k_feature, key_high, key_low),
        3 * unit,
        name="key_out",
    )
    return (
        jnp.concatenate(query_grads, axis=1),
        grad_keys,
        grad_values,
        q_sum.reshape(heads, width, half),
        k_sum,
    )


def solution(mesh):
    placed = (
        P("ctx", "head"),
        P("ctx", None),
        P("ctx", None),
        P("ctx", "head"),
        P("ctx"),
        P(),
        P("head", None, None),
        P(),
    )
    return jax.shard_map(
        on_device,
        mesh=mesh,
        in_specs=placed,
        out_specs=(
            P("ctx", "head"),
            P(("ctx", "head"), None),
            P(("ctx", "head"), None),
            P("head", None, None),
            P(),
        ),
        check_vma=False,
    )
```

```python
import functools

import jax
import jax.numpy as jnp
from jax import lax
from jax.experimental import pallas as pl
from jax.experimental.pallas import tpu as pltpu
from jax.sharding import PartitionSpec as P


F32 = jnp.float32
BF16 = jnp.bfloat16
NN = ((1,), (0,))
NT = ((1,), (1,))
TN = ((0,), (0,))


def split(x):
    high = x.astype(BF16)
    return high, (x - high.astype(F32)).astype(BF16)


def joined(pair):
    return pair[0].astype(F32) + pair[1].astype(F32)


def raw_dot(a, b, dims):
    return lax.dot_general(a, b, (dims, ((), ())), preferred_element_type=F32)


def dot3(a, b, dims):
    return raw_dot(a[0], b[0], dims) + (raw_dot(a[0], b[1], dims) + raw_dot(a[1], b[0], dims))


def dot_exact(a, b, dims):
    return lax.dot_general(
        a, b, (dims, ((), ())), precision=lax.Precision.HIGHEST, preferred_element_type=F32
    )


def softmaxes(logits):
    upper = jnp.exp(logits - jnp.max(logits, axis=-1, keepdims=True))
    lower = jnp.exp(jnp.min(logits, axis=-1, keepdims=True) - logits)
    return (
        upper / jnp.sum(upper, axis=-1, keepdims=True),
        lower / jnp.sum(lower, axis=-1, keepdims=True),
    )


def logit_grad(features, grad):
    half = features.shape[1] // 2
    upper, lower = features[:, :half], features[:, half:]
    a, b = grad[:, :half], grad[:, half:]
    up = upper * (a - jnp.sum(upper * a, axis=-1, keepdims=True))
    return up - lower * (b - jnp.sum(lower * b, axis=-1, keepdims=True))


def digits_of(count):
    found, base = [], 1
    while base < count:
        radix = 4 if (count // base) % 4 == 0 else 2
        found.append((base, radix))
        base *= radix
    return found


def exchange(values, axis, base, radix):
    count = lax.axis_size(axis)
    received = []
    for m in range(1, radix):
        value = values[m - 1] if isinstance(values, (list, tuple)) else values
        received.append(
            lax.ppermute(value, axis, [(i, i ^ (base * m)) for i in range(count)])
        )
    return received


def grant(size):
    return (4 << 20) + 3 * size


def call(body, outs, args, flops=0, in_specs=None, out_specs=None, scratch=(), aliases=None):
    size = sum(4 * a.size for a in args) + sum(4 * o.size for o in outs)
    kwargs = {}
    if in_specs is not None:
        kwargs["in_specs"] = in_specs
    if out_specs is not None:
        kwargs["out_specs"] = out_specs
        kwargs["grid"] = (1,)
    return pl.pallas_call(
        body,
        out_shape=outs,
        scratch_shapes=scratch,
        input_output_aliases=aliases or {},
        cost_estimate=pl.CostEstimate(flops=flops, bytes_accessed=size, transcendentals=0),
        compiler_params=pltpu.CompilerParams(vmem_limit_bytes=grant(size)),
        **kwargs,
    )(*args)


def whole(shape):
    return pl.BlockSpec(shape, lambda i: (0,) * len(shape))


def out(shape, dtype=F32):
    return jax.ShapeDtypeStruct(shape, dtype)


def put_message(ref, state, totals):
    rows, half = state.shape[0], state.shape[1] // 2
    ref[0:rows] = state[:, :half]
    ref[rows : 2 * rows] = state[:, half:]
    first = lax.broadcasted_iota(jnp.int32, (8, half), 0) < 4
    ref[2 * rows : 2 * rows + 8] = jnp.where(first, totals[:, :half], totals[:, half:])


def take_totals(piece, rows):
    return jnp.concatenate(
        [piece[2 * rows : 2 * rows + 1], piece[2 * rows + 4 : 2 * rows + 5]], axis=1
    )


def put_state(piece, scratch, rows, owner):
    half = piece.shape[1]
    at = pl.ds(pl.multiple_of(owner * rows, 8), rows)
    scratch[at, :half] = piece[0:rows]
    scratch[at, half:] = piece[rows : 2 * rows]


def key_body(
    share, keys_hbm, values_hbm, weight_hbm, feat_high, feat_low, message,
    scratch, keys, values, weight, arrived,
):
    mine = lax.axis_index("head")
    pairs = [(keys_hbm, keys), (weight_hbm, weight), (values_hbm, values)]
    copies = [
        pltpu.make_async_copy(source, target, arrived.at[n])
        for n, (source, target) in enumerate(pairs)
    ]
    for copy in copies:
        copy.start()
    copies[0].wait()
    copies[1].wait()
    upper, lower = softmaxes(dot_exact(keys[...], weight[...], NN))
    feat = split(jnp.concatenate([upper, lower], axis=1))
    feat_high[...] = feat[0]
    feat_low[...] = feat[1]
    ones = jnp.ones((8, feat[0].shape[0]), BF16)
    totals = raw_dot(ones, feat[0], NN) + raw_dot(ones, feat[1], NN)
    copies[2].wait()
    scratch[...] = dot3(split(values[...]), feat, TN)
    state = scratch[pl.ds(pl.multiple_of(mine * share, 8), share), :]
    put_message(message, state, totals)


def causal(size):
    row = lax.broadcasted_iota(jnp.int32, (size, size), 0)
    col = lax.broadcasted_iota(jnp.int32, (size, size), 1)
    return row >= col


def query_body(
    block, queries, weight, values, key_high, key_low,
    feat_high, feat_low, score_high, score_low, numer, norm,
):
    upper, lower = softmaxes(dot_exact(queries[...], weight[0], NN))
    feat = split(jnp.concatenate([upper, lower], axis=1))
    feat_high[...] = feat[0]
    feat_low[...] = feat[1]
    rows, width = values.shape
    extended = split(jnp.concatenate([values[...], jnp.ones((rows, width), F32)], axis=1))
    mask = causal(block)
    for i in range(rows // block):
        at = slice(i * block, (i + 1) * block)
        total = None
        for j in range(i + 1):
            past = slice(j * block, (j + 1) * block)
            scores = dot3((feat[0][at], feat[1][at]), (key_high[past], key_low[past]), NT)
            if i == j:
                scores = jnp.where(mask, scores, 0.0)
            pair = split(scores)
            score_high[at, past] = pair[0]
            score_low[at, past] = pair[1]
            term = dot3(pair, (extended[0][past], extended[1][past]), NN)
            total = term if total is None else total + term
        numer[at] = total[:, :width]
        norm[at] = total[:, width:]


def scan_body(base, radix, local, *refs):
    received, (total, before) = refs[: radix - 1], refs[radix - 1 :]
    mine = (lax.axis_index("ctx") // base) % radix
    whole_sum, earlier = local[...], jnp.zeros(local.shape, F32)
    for m, piece in enumerate(received, 1):
        value = piece[...]
        whole_sum = whole_sum + value
        earlier = earlier + jnp.where((mine ^ m) < mine, value, 0.0)
    total[...] = whole_sum
    before[...] = earlier


def scan_last_body(base, radix, before, *refs):
    received, (result,) = refs[: radix - 1], refs[radix - 1 :]
    mine = (lax.axis_index("ctx") // base) % radix
    earlier = before[...]
    for m, piece in enumerate(received, 1):
        earlier = earlier + jnp.where((mine ^ m) < mine, piece[...], 0.0)
    result[...] = earlier


def inter_body(heads, peers, share, *refs):
    pieces, refs = refs[:peers], refs[peers:]
    feats, refs = [refs[2 * h : 2 * h + 2] for h in range(heads)], refs[2 * heads :]
    locals_, refs = [refs[2 * h : 2 * h + 2] for h in range(heads)], refs[2 * heads :]
    scaled, refs = refs[0], refs[1:]
    state_high, state_low = refs[:2]
    refs = refs[2:]
    grads, refs = refs[:heads], refs[heads:]
    messages, refs = refs[:peers], refs[peers:]
    scratch, = refs
    mine = lax.axis_index("head")
    for m, piece in enumerate(pieces):
        put_state(piece, scratch, share, mine ^ m)
    state = scratch[...]
    width = state.shape[0]
    totals = jnp.broadcast_to(take_totals(pieces[0], share), state.shape)
    extended = split(jnp.concatenate([state, totals], axis=0))
    state_high[...] = extended[0]
    state_low[...] = extended[1]
    carried = None
    for h in range(heads):
        feat = (feats[h][0][...], feats[h][1][...])
        inter = dot3(feat, extended, NT)
        numer = locals_[h][0][...] + inter[:, :width]
        norm = locals_[h][1][...] + inter[:, width:]
        mine_scaled = scaled[:, h * width : (h + 1) * width]
        grad_numer = mine_scaled / norm
        along = jnp.sum(mine_scaled * (numer / norm), axis=1, keepdims=True)
        both = jnp.concatenate([grad_numer, -(along / norm)], axis=1)
        grads[h][...] = both
        term = dot3(split(both), feat, TN)
        carried = term if carried is None else carried + term
    scratch[...] = carried[:width]
    for m, message in enumerate(messages):
        part = scratch[pl.ds(pl.multiple_of((mine ^ m) * share, 8), share), :]
        put_message(message, part, carried[width : width + 8])


def query_grad_body(
    block, first, queries, weight, values, key_high, key_low, feat_high, feat_low,
    score_high, score_low, grads, state_high, state_low, *refs,
):
    earlier, (grad_input, grad_weight, grad_key) = refs[1:-3], refs[-3:]
    rows, width = values.shape
    wide = key_high.shape[1]
    both = grads[...]
    numer = split(both[:, :width])
    scale = 1.0 / width
    extended = split(jnp.concatenate([both[:, :width], both[:, width:] * scale], axis=1))
    value_pair = split(values[...])
    feat = (feat_high[...], feat_low[...])
    state = (state_high[...], state_low[...])
    mask = causal(block)
    count = rows // block
    key_sums, value_sums, logit_parts = [None] * count, [None] * count, []
    cut = lambda pair, at: (pair[0][at], pair[1][at])
    for i in range(count):
        at = slice(i * block, (i + 1) * block)
        norm_part = both[at, width:]
        norm_part = jnp.concatenate([norm_part] * (block // width), axis=1)
        grad_query = dot3(cut(extended, at), state, NN)
        for j in range(i + 1):
            past = slice(j * block, (j + 1) * block)
            grad_scores = dot3(cut(numer, at), cut(value_pair, past), NT) + norm_part
            if i == j:
                grad_scores = jnp.where(mask, grad_scores, 0.0)
            pair = split(grad_scores)
            keys = (key_high[past], key_low[past])
            grad_query = grad_query + dot3(pair, keys, NN)
            key_term = dot3(pair, cut(feat, at), TN)
            value_term = dot3((score_high[at, past], score_low[at, past]), cut(numer, at), TN)
            key_sums[j] = key_term if key_sums[j] is None else key_sums[j] + key_term
            value_sums[j] = value_term if value_sums[j] is None else value_sums[j] + value_term
        logit_parts.append(logit_grad(joined(cut(feat, at)), grad_query))
    grad_logits = split(jnp.concatenate(logit_parts, axis=0))
    grad_input[...] = dot3(grad_logits, split(weight[0]), NT)
    grad_weight[...] = dot3(split(queries[...]), grad_logits, TN)
    for j in range(count):
        past = slice(j * block, (j + 1) * block)
        if first:
            grad_key[past, :wide] = key_sums[j]
            grad_key[past, wide:] = value_sums[j]
        else:
            grad_key[past, :wide] = earlier[0][past, :wide] + key_sums[j]
            grad_key[past, wide:] = earlier[0][past, wide:] + value_sums[j]


def sum_body(*refs):
    total = refs[0][...]
    for piece in refs[1:-1]:
        total = total + piece[...]
    refs[-1][...] = total


def suffix_weight_body(base, radix, above, heads, local, *refs):
    received, refs = refs[: above - 1], refs[above - 1 :]
    weights, (later, kept, *messages) = refs[:heads], refs[heads:]
    scratch = messages.pop()
    mine = (lax.axis_index("ctx") // base) % radix
    upper = (lax.axis_index("ctx") // (base * radix)) % above
    size = local.shape[0]
    width = weights[0].shape[0]
    shard = heads * width // radix
    for h, weight in enumerate(weights):
        scratch[h * width : (h + 1) * width] = weight[...]
    total = jnp.zeros(local.shape, F32)
    for m, piece in enumerate(received, 1):
        total = total + jnp.where((upper ^ m) > upper, piece[...], 0.0)
    later[...] = total
    rows = lambda m: pl.ds(pl.multiple_of((mine ^ m) * shard, 8), shard)
    kept[...] = scratch[rows(0), :]
    for m, message in enumerate(messages, 1):
        message[0:size] = total + jnp.where(mine > (mine ^ m), local[...], 0.0)
        message[size : size + shard] = scratch[rows(m), :]


def suffix_last_body(later, kept, *refs):
    received, (result, shard) = refs[:-2], refs[-2:]
    size = later.shape[0]
    total, sums = later[...], kept[...]
    for piece in received:
        total = total + piece[0:size]
        sums = sums + piece[size : size + sums.shape[0]]
    result[...] = total
    shard[...] = sums


def key_grad_body(share, piece, inner, values, keys, key_high, key_low, *refs):
    logit_ref, state_high, state_low, *parts, scratch, weights = refs
    mine = lax.axis_index("head")
    scratch[...] = jnp.zeros(scratch.shape, F32)
    put_state(piece, scratch, share, mine)
    state = split(scratch[...])
    state_high[...] = state[0]
    state_low[...] = state[1]
    totals = jnp.where(mine == 0, take_totals(piece, share), 0.0)
    wide = key_high.shape[1]
    grad = dot3(split(values[...]), state, NN) + totals + inner[:, :wide]
    feat = (key_high[...], key_low[...])
    grad_logits = logit_grad(joined(feat), grad)
    logit_ref[...] = grad_logits
    weights[...] = dot3(split(keys[...]), split(grad_logits), TN)
    rows = parts[0].shape[0]
    for m, target in enumerate(parts):
        target[...] = weights[pl.ds(pl.multiple_of((mine ^ m) * rows, 8), rows), :]


def key_out_body(part, logits, inner, state_high, state_low, weight, key_high, key_low, *refs):
    parts, both = refs[:-1], refs[-1]
    mine = lax.axis_index("head")
    width = weight.shape[0]
    wide = key_high.shape[1]
    feat = (key_high[...], key_low[...])
    both[:, :width] = dot3(split(logits[...]), split(weight[...]), NT)
    both[:, width:] = inner[:, wide:] + dot3(feat, (state_high[...], state_low[...]), NT)
    for m, target in enumerate(parts):
        target[...] = both[pl.ds(pl.multiple_of((mine ^ m) * part, 8), part), :]


def key_sum_body(*refs):
    pieces, (grad_key, grad_value) = refs[:-2], refs[-2:]
    total = pieces[0][...]
    for piece in pieces[1:]:
        total = total + piece[...]
    width = grad_key.shape[1]
    grad_key[...] = total[:, :width]
    grad_value[...] = total[:, width:]


def weight_message_body(*refs):
    parts, shard, message = refs[:-2], refs[-2], refs[-1]
    total = parts[0][...]
    for piece in parts[1:]:
        total = total + piece[...]
    rows = total.shape[0]
    message[0:rows] = total
    message[rows:] = shard[...]


def weight_last_body(base, radix, rows, local, *refs):
    received, (share, gathered) = refs[: radix - 1], refs[radix - 1 :]
    mine = (lax.axis_index("ctx") // base) % radix
    total = local[0:rows]
    shard = local.shape[0] - rows
    gathered[pl.ds(pl.multiple_of(mine * shard, 8), shard), :] = local[rows:]
    for m, piece in enumerate(received, 1):
        total = total + piece[0:rows]
        at = pl.ds(pl.multiple_of((mine ^ m) * shard, 8), shard)
        gathered[at, :] = piece[rows:]
    share[...] = total


def gather_body(rows, *refs):
    pieces, result = refs[:-1], refs[-1]
    mine = lax.axis_index("head")
    for m, piece in enumerate(pieces):
        result[pl.ds(pl.multiple_of((mine ^ m) * rows, 8), rows), :] = piece[...]


def backward(queries, keys, values, cotangent, source_ids, source_weights, q_feature, k_feature):
    heads, width, half = q_feature.shape
    wide = 2 * half
    rows = queries.shape[0]
    peers = lax.axis_size("head")
    share = width // peers
    part = rows // peers
    block = min(256, rows)
    digits = digits_of(lax.axis_size("ctx"))
    message = (2 * share + 8, half)
    bind = functools.partial
    unit = 2 * rows * width * wide
    hbm = pl.BlockSpec(memory_space=pltpu.HBM)

    source_index = lax.broadcasted_iota(jnp.int32, (1, source_weights.shape[0]), 1)
    lookup = source_ids[:, None] == source_index
    weight = jnp.sum(jnp.where(lookup, source_weights[None, :], 0.0), axis=1)
    scaled = cotangent * weight[:, None]

    feat_shape = out((rows, wide), BF16)
    key_high, key_low, local = call(
        bind(key_body, share),
        [feat_shape, feat_shape, out(message)],
        (keys, values, k_feature),
        6 * unit,
        [hbm] * 3,
        scratch=[
            pltpu.VMEM((width, wide), F32),
            pltpu.VMEM(keys.shape, F32),
            pltpu.VMEM(values.shape, F32),
            pltpu.VMEM(k_feature.shape, F32),
            pltpu.SemaphoreType.DMA((3,)),
        ],
    )

    before, total = None, local
    for place, (base, radix) in enumerate(digits):
        received = exchange(total, "ctx", base, radix)
        if place == 0:
            total, before = call(
                bind(scan_body, base, radix), [out(message)] * 2, (total, *received)
            )
        else:
            (before,) = call(bind(scan_last_body, base, radix), [out(message)], (before, *received))
            if place + 1 < len(digits):
                total = sum(received, total)
    prefix = [before] + exchange(before, "head", 1, peers)

    def head_specs(h):
        return [
            pl.BlockSpec((rows, width), lambda i: (0, h)),
            pl.BlockSpec((1, width, half), lambda i: (h, 0, 0)),
        ]

    feats, scores, inner = [], [], []
    for h in range(heads):
        args = (queries, q_feature, values, key_high, key_low)
        outs = (
            [feat_shape] * 2 + [out((rows, rows), BF16)] * 2 + [out((rows, width))] * 2
        )
        results = call(
            bind(query_body, block),
            outs,
            args,
            9 * unit,
            head_specs(h) + [whole(a.shape) for a in args[2:]],
            [whole(o.shape) for o in outs],
        )
        feats.append(results[0:2])
        scores.append(results[2:4])
        inner.append(results[4:6])

    results = call(
        bind(inter_body, heads, peers, share),
        [out((2 * width, wide), BF16)] * 2
        + [out((rows, 2 * width))] * heads
        + [out(message)] * peers,
        (
            *prefix,
            *[x for pair in feats for x in pair],
            *[x for pair in inner for x in pair],
            scaled,
        ),
        12 * heads * unit,
        scratch=[pltpu.VMEM((width, wide), F32)],
    )
    state, results = results[:2], results[2:]
    grads, results = results[:heads], results[heads:]
    sends = exchange(results[1:], "head", 1, peers)
    (carried,) = call(sum_body, [out(message)], (results[0], *sends))

    weight_grads = []
    grad_queries = key_inner = None
    for h in range(heads):
        args = [
            queries, q_feature, values, key_high, key_low, *feats[h], *scores[h], grads[h], *state,
        ]
        outs = [
            out((rows, heads * width)), out((width, half)), out((rows, wide + width)),
        ]
        specs = head_specs(h) + [whole(a.shape) for a in args[2:]]
        aliases = {}
        if h > 0:
            aliases = {len(args): 0}
            args += [grad_queries, key_inner]
            specs += [pl.BlockSpec(memory_space=pl.ANY), whole(key_inner.shape)]
        grad_queries, grad_weight, key_inner = call(
            bind(query_grad_body, block, h == 0),
            outs,
            args,
            15 * unit,
            specs,
            [head_specs(h)[0]] + [whole(o.shape) for o in outs[1:]],
            aliases=aliases,
        )
        weight_grads.append(grad_weight)

    later, messages = None, carried
    base_low, radix_low = digits[0]
    shard = heads * width // radix_low
    for place in range(len(digits) - 1, 0, -1):
        base, radix = digits[place]
        received = exchange(messages, "ctx", base, radix)
        below_base, below_radix = digits[place - 1]
        if place == 1 and len(digits) == 2:
            results = call(
                bind(suffix_weight_body, base_low, radix_low, radix, heads),
                [out(message), out((shard, half))]
                + [out((message[0] + shard, half))] * (radix_low - 1),
                (carried, *received, *weight_grads),
                scratch=[pltpu.VMEM((heads * width, half), F32)],
            )
            later, kept, messages = results[0], results[1], results[2:]
        else:
            mine = (lax.axis_index("ctx") // base) % radix
            if place == len(digits) - 1:
                later = sum(jnp.where((mine ^ m) > mine, r, 0.0) for m, r in enumerate(received, 1))
            else:
                later = sum(received, later)
            below = (lax.axis_index("ctx") // below_base) % below_radix
            messages = [
                later + jnp.where(below > (below ^ m), carried, 0.0) for m in range(1, below_radix)
            ]
            if place == 1:
                stacked = jnp.concatenate(weight_grads, axis=0)
                cut = lambda m: lax.dynamic_slice_in_dim(stacked, (below ^ m) * shard, shard, 0)
                kept = cut(0)
                messages = [
                    jnp.concatenate([part_message, cut(m)], axis=0)
                    for m, part_message in enumerate(messages, 1)
                ]
    received = exchange(messages, "ctx", base_low, radix_low)
    later, q_shard = call(
        suffix_last_body, [out(message), out((shard, half))], (later, kept, *received)
    )

    weight_rows = width // peers
    results = call(
        bind(key_grad_body, share),
        [out((rows, half))]
        + [out((width, wide), BF16)] * 2
        + [out((weight_rows, half))] * peers,
        (later, key_inner, values, keys, key_high, key_low),
        6 * unit,
        scratch=[pltpu.VMEM((width, wide), F32), pltpu.VMEM((width, half), F32)],
    )
    key_logits, later_high, later_low = results[:3]
    weight_parts = results[3:]
    weight_parts = [weight_parts[0]] + exchange(weight_parts[1:], "head", 1, peers)
    (total,) = call(
        weight_message_body, [out((weight_rows + shard, half))], (*weight_parts, q_shard)
    )
    key_parts = call(
        bind(key_out_body, part),
        [out((part, 2 * width))] * peers,
        (key_logits, key_inner, later_high, later_low, k_feature, key_high, key_low),
        6 * unit,
        scratch=[pltpu.VMEM((rows, 2 * width), F32)],
    )
    key_parts = [key_parts[0]] + exchange(key_parts[1:], "head", 1, peers)
    grad_keys, grad_values = call(key_sum_body, [out((part, width))] * 2, key_parts)
    for place in range(len(digits) - 1, 0, -1):
        base, radix = digits[place]
        received = exchange(total, "ctx", base, radix)
        (total,) = call(sum_body, [out(total.shape)], (total, *received))
    received = exchange(total, "ctx", base_low, radix_low)
    k_share, q_sum = call(
        bind(weight_last_body, base_low, radix_low, weight_rows),
        [out((weight_rows, half)), out((heads * width, half))],
        (total, *received),
    )
    shares = [k_share] + exchange(k_share, "head", 1, peers)
    (k_sum,) = call(bind(gather_body, weight_rows), [out((width, half))], shares)
    return (
        grad_queries,
        grad_keys,
        grad_values,
        q_sum.reshape(heads, width, half),
        k_sum,
    )


def solution(mesh):
    placed = (
        P("ctx", "head"),
        P("ctx", None),
        P("ctx", None),
        P("ctx", "head"),
        P("ctx"),
        P(),
        P("head", None, None),
        P(),
    )
    return jax.shard_map(
        backward,
        mesh=mesh,
        in_specs=placed,
        out_specs=(
            P("ctx", "head"),
            P(("ctx", "head"), None),
            P(("ctx", "head"), None),
            P("head", None, None),
            P(),
        ),
        check_vma=False,
    )
```

```python
import functools

import jax
import jax.numpy as jnp
from jax import lax
from jax.experimental import pallas as pl
from jax.experimental.pallas import tpu as pltpu
from jax.sharding import PartitionSpec as P


F32 = jnp.float32
BF16 = jnp.bfloat16
NN = ((1,), (0,))
NT = ((1,), (1,))
TN = ((0,), (0,))


def split(x):
    high = x.astype(BF16)
    return high, (x - high.astype(F32)).astype(BF16)


def joined(pair):
    return pair[0].astype(F32) + pair[1].astype(F32)


def raw_dot(a, b, dims):
    return lax.dot_general(a, b, (dims, ((), ())), preferred_element_type=F32)


def dot3(a, b, dims):
    return raw_dot(a[0], b[0], dims) + (raw_dot(a[0], b[1], dims) + raw_dot(a[1], b[0], dims))


def dot_exact(a, b, dims):
    return lax.dot_general(
        a, b, (dims, ((), ())), precision=lax.Precision.HIGHEST, preferred_element_type=F32
    )


def softmaxes(logits):
    upper = jnp.exp(logits - jnp.max(logits, axis=-1, keepdims=True))
    lower = jnp.exp(jnp.min(logits, axis=-1, keepdims=True) - logits)
    return (
        upper / jnp.sum(upper, axis=-1, keepdims=True),
        lower / jnp.sum(lower, axis=-1, keepdims=True),
    )


def logit_grad(features, grad):
    half = features.shape[1] // 2
    upper, lower = features[:, :half], features[:, half:]
    a, b = grad[:, :half], grad[:, half:]
    up = upper * (a - jnp.sum(upper * a, axis=-1, keepdims=True))
    return up - lower * (b - jnp.sum(lower * b, axis=-1, keepdims=True))


def digits_of(count):
    found, base = [], 1
    while base < count:
        radix = 4 if (count // base) % 4 == 0 else 2
        found.append((base, radix))
        base *= radix
    return found


def rounds_of(count, peers, rising):
    digits = digits_of(count)
    radices = [radix for _, radix in digits]
    joint = peers % 2 == 0 and radices == radices[::-1]
    even = digits if rising else digits[::-1]
    odd = even[::-1] if joint else even
    ups = (rising, (not rising) if joint else rising)
    return [(e[0], o[0], e[1]) for e, o in zip(even, odd)], ups


def position(step):
    even, odd, radix = step
    index = lax.axis_index("ctx")
    is_odd = lax.axis_index("head") % 2 == 1
    return jnp.where(is_odd, (index // odd) % radix, (index // even) % radix)


def is_up(ups):
    return (lax.axis_index("head") % 2 == 1) == ups[1] if ups[0] != ups[1] else ups[0]


def swap(values, step):
    even, odd, radix = step
    count, peers = lax.axis_size("ctx"), lax.axis_size("head")
    received = []
    for m in range(1, radix):
        value = values[m - 1] if isinstance(values, (list, tuple)) else values
        pairs = [
            (i * peers + h, (i ^ (m * (odd if h % 2 else even))) * peers + h)
            for i in range(count)
            for h in range(peers)
        ]
        received.append(lax.ppermute(value, ("ctx", "head"), pairs))
    return received


def exchange(values, peers):
    received = []
    for m in range(1, peers):
        value = values[m - 1] if isinstance(values, (list, tuple)) else values
        received.append(lax.ppermute(value, "head", [(i, i ^ m) for i in range(peers)]))
    return received


def grant(size):
    return (4 << 20) + 3 * size


def call(body, outs, args, flops=0, in_specs=None, out_specs=None, scratch=()):
    size = sum(4 * a.size for a in args) + sum(4 * o.size for o in outs)
    kwargs = {}
    if in_specs is not None:
        kwargs["in_specs"] = in_specs
    if out_specs is not None:
        kwargs["out_specs"] = out_specs
        kwargs["grid"] = (1,)
    return pl.pallas_call(
        body,
        out_shape=outs,
        scratch_shapes=scratch,
        cost_estimate=pl.CostEstimate(flops=flops, bytes_accessed=size, transcendentals=0),
        compiler_params=pltpu.CompilerParams(vmem_limit_bytes=grant(size)),
        **kwargs,
    )(*args)


def whole(shape):
    return pl.BlockSpec(shape, lambda i: (0,) * len(shape))


def out(shape, dtype=F32):
    return jax.ShapeDtypeStruct(shape, dtype)


def put_message(ref, state, totals):
    rows, half = state.shape[0], state.shape[1] // 2
    ref[0:rows] = state[:, :half]
    ref[rows : 2 * rows] = state[:, half:]
    first = lax.broadcasted_iota(jnp.int32, (8, half), 0) < 4
    ref[2 * rows : 2 * rows + 8] = jnp.where(first, totals[:, :half], totals[:, half:])


def take_totals(piece, rows):
    return jnp.concatenate(
        [piece[2 * rows : 2 * rows + 1], piece[2 * rows + 4 : 2 * rows + 5]], axis=1
    )


def put_state(piece, scratch, rows, owner):
    half = piece.shape[1]
    at = pl.ds(pl.multiple_of(owner * rows, 8), rows)
    scratch[at, :half] = piece[0:rows]
    scratch[at, half:] = piece[rows : 2 * rows]


def key_body(
    share, keys_hbm, values_hbm, weight_hbm, feat_high, feat_low, message,
    scratch, keys, values, weight, arrived,
):
    mine = lax.axis_index("head")
    pairs = [(keys_hbm, keys), (weight_hbm, weight), (values_hbm, values)]
    copies = [
        pltpu.make_async_copy(source, target, arrived.at[n])
        for n, (source, target) in enumerate(pairs)
    ]
    for copy in copies:
        copy.start()
    copies[0].wait()
    copies[1].wait()
    upper, lower = softmaxes(dot_exact(keys[...], weight[...], NN))
    feat = split(jnp.concatenate([upper, lower], axis=1))
    feat_high[...] = feat[0]
    feat_low[...] = feat[1]
    ones = jnp.ones((8, feat[0].shape[0]), BF16)
    totals = raw_dot(ones, feat[0], NN) + raw_dot(ones, feat[1], NN)
    copies[2].wait()
    scratch[...] = dot3(split(values[...]), feat, TN)
    state = scratch[pl.ds(pl.multiple_of(mine * share, 8), share), :]
    put_message(message, state, totals)


def causal(size):
    row = lax.broadcasted_iota(jnp.int32, (size, size), 0)
    col = lax.broadcasted_iota(jnp.int32, (size, size), 1)
    return row >= col


def query_body(
    block, queries, weight, values, key_high, key_low,
    feat_high, feat_low, score_high, score_low, numer, norm,
):
    upper, lower = softmaxes(dot_exact(queries[...], weight[0], NN))
    feat = split(jnp.concatenate([upper, lower], axis=1))
    feat_high[...] = feat[0]
    feat_low[...] = feat[1]
    rows, width = values.shape
    extended = split(jnp.concatenate([values[...], jnp.ones((rows, width), F32)], axis=1))
    mask = causal(block)
    for i in range(rows // block):
        at = slice(i * block, (i + 1) * block)
        total = None
        for j in range(i + 1):
            past = slice(j * block, (j + 1) * block)
            scores = dot3((feat[0][at], feat[1][at]), (key_high[past], key_low[past]), NT)
            if i == j:
                scores = jnp.where(mask, scores, 0.0)
            pair = split(scores)
            score_high[at, past] = pair[0]
            score_low[at, past] = pair[1]
            term = dot3(pair, (extended[0][past], extended[1][past]), NN)
            total = term if total is None else total + term
        numer[at] = total[:, :width]
        norm[at] = total[:, width:]


def counts(prefix, mine, m):
    return (mine ^ m) < mine if prefix else (mine ^ m) > mine


def step_body(now, after, ups, prefix, first, final, heads, local, *refs):
    held, refs = ([], refs) if first else (refs[:2], refs[2:])
    received, refs = refs[: now[2] - 1], refs[now[2] - 1 :]
    weights, refs = refs[:heads], refs[heads:]
    up, mine, then = is_up(ups), position(now), position(after)
    own = local[...]
    size = own.shape[0]
    total = own if first else held[1][...]
    part = jnp.zeros(own.shape, F32) if first else held[0][...]
    for m, piece in enumerate(received, 1):
        value = piece[...]
        total = total + value
        take = counts(prefix, mine, m)
        if not first:
            take = jnp.logical_or(take, jnp.logical_not(up))
        part = part + jnp.where(take, value, 0.0)
    refs[0][...] = part
    if not final:
        refs[1][...] = total
    refs = refs[1 if final else 2 :]
    if heads:
        scratch, kept, refs = refs[-1], refs[0], refs[1:-1]
        width = weights[0].shape[0]
        shard = kept.shape[0]
        for h, weight in enumerate(weights):
            scratch[h * width : (h + 1) * width] = weight[...]
        rows = lambda m: pl.ds(pl.multiple_of((then ^ m) * shard, 8), shard)
        kept[...] = scratch[rows(0), :]
    for m, message in enumerate(refs, 1):
        falling = part + jnp.where(counts(prefix, then, m), 0.0, own)
        message[0:size] = jnp.where(up, total, falling)
        if heads:
            message[size:] = scratch[rows(m), :]


def last_body(now, ups, prefix, part, *refs):
    received, refs = refs[: now[2] - 1], refs[now[2] - 1 :]
    up, mine = is_up(ups), position(now)
    total = part[...]
    size = total.shape[0]
    for m, piece in enumerate(received, 1):
        take = jnp.logical_or(counts(prefix, mine, m), jnp.logical_not(up))
        total = total + jnp.where(take, piece[0:size], 0.0)
    refs[-1][...] = total


def shard_sum_body(size, kept, *refs):
    total = kept[...]
    for piece in refs[:-1]:
        total = total + piece[size:]
    refs[-1][...] = total


def inter_body(heads, peers, share, *refs):
    pieces, refs = refs[:peers], refs[peers:]
    feats, refs = [refs[2 * h : 2 * h + 2] for h in range(heads)], refs[2 * heads :]
    locals_, refs = [refs[2 * h : 2 * h + 2] for h in range(heads)], refs[2 * heads :]
    scaled, refs = refs[0], refs[1:]
    state_high, state_low = refs[:2]
    refs = refs[2:]
    grads, refs = refs[:heads], refs[heads:]
    messages, refs = refs[:peers], refs[peers:]
    scratch, = refs
    mine = lax.axis_index("head")
    for m, piece in enumerate(pieces):
        put_state(piece, scratch, share, mine ^ m)
    state = scratch[...]
    width = state.shape[0]
    totals = jnp.broadcast_to(take_totals(pieces[0], share), state.shape)
    extended = split(jnp.concatenate([state, totals], axis=0))
    state_high[...] = extended[0]
    state_low[...] = extended[1]
    carried = None
    for h in range(heads):
        feat = (feats[h][0][...], feats[h][1][...])
        inter = dot3(feat, extended, NT)
        numer = locals_[h][0][...] + inter[:, :width]
        norm = locals_[h][1][...] + inter[:, width:]
        mine_scaled = scaled[:, h * width : (h + 1) * width]
        grad_numer = mine_scaled / norm
        along = jnp.sum(mine_scaled * (numer / norm), axis=1, keepdims=True)
        both = jnp.concatenate([grad_numer, -(along / norm)], axis=1)
        grads[h][...] = both
        term = dot3(split(both), feat, TN)
        carried = term if carried is None else carried + term
    scratch[...] = carried[:width]
    for m, message in enumerate(messages):
        part = scratch[pl.ds(pl.multiple_of((mine ^ m) * share, 8), share), :]
        put_message(message, part, carried[width : width + 8])


def query_grad_body(
    block, first, queries, values, key_high, key_low, feat_high, feat_low,
    score_high, score_low, grads, state_high, state_low, *refs,
):
    earlier, (logit_ref, grad_weight, grad_key) = refs[:-3], refs[-3:]
    rows, width = values.shape
    wide = key_high.shape[1]
    both = grads[...]
    numer = split(both[:, :width])
    scale = 1.0 / width
    extended = split(jnp.concatenate([both[:, :width], both[:, width:] * scale], axis=1))
    value_pair = split(values[...])
    feat = (feat_high[...], feat_low[...])
    state = (state_high[...], state_low[...])
    mask = causal(block)
    count = rows // block
    key_sums, value_sums, logit_parts = [None] * count, [None] * count, []
    cut = lambda pair, at: (pair[0][at], pair[1][at])
    for i in range(count):
        at = slice(i * block, (i + 1) * block)
        norm_part = both[at, width:]
        norm_part = jnp.concatenate([norm_part] * (block // width), axis=1)
        grad_query = dot3(cut(extended, at), state, NN)
        for j in range(i + 1):
            past = slice(j * block, (j + 1) * block)
            grad_scores = dot3(cut(numer, at), cut(value_pair, past), NT) + norm_part
            if i == j:
                grad_scores = jnp.where(mask, grad_scores, 0.0)
            pair = split(grad_scores)
            keys = (key_high[past], key_low[past])
            grad_query = grad_query + dot3(pair, keys, NN)
            key_term = dot3(pair, cut(feat, at), TN)
            value_term = dot3((score_high[at, past], score_low[at, past]), cut(numer, at), TN)
            key_sums[j] = key_term if key_sums[j] is None else key_sums[j] + key_term
            value_sums[j] = value_term if value_sums[j] is None else value_sums[j] + value_term
        logit_parts.append(logit_grad(joined(cut(feat, at)), grad_query))
    grad_logits = jnp.concatenate(logit_parts, axis=0)
    logit_ref[...] = grad_logits
    grad_weight[...] = dot3(split(queries[...]), split(grad_logits), TN)
    for j in range(count):
        past = slice(j * block, (j + 1) * block)
        if first:
            grad_key[past, :wide] = key_sums[j]
            grad_key[past, wide:] = value_sums[j]
        else:
            grad_key[past, :wide] = earlier[0][past, :wide] + key_sums[j]
            grad_key[past, wide:] = earlier[0][past, wide:] + value_sums[j]


def query_out_body(heads, weights, *refs):
    logits, result = refs[:heads], refs[heads]
    width = weights.shape[1]
    for h in range(heads):
        result[:, h * width : (h + 1) * width] = dot3(
            split(logits[h][...]), split(weights[h]), NT
        )


def sum_body(*refs):
    total = refs[0][...]
    for piece in refs[1:-1]:
        total = total + piece[...]
    refs[-1][...] = total


def key_grad_body(share, piece, inner, values, keys, key_high, key_low, *refs):
    logit_ref, state_high, state_low, *parts, scratch, weights = refs
    mine = lax.axis_index("head")
    scratch[...] = jnp.zeros(scratch.shape, F32)
    put_state(piece, scratch, share, mine)
    state = split(scratch[...])
    state_high[...] = state[0]
    state_low[...] = state[1]
    totals = jnp.where(mine == 0, take_totals(piece, share), 0.0)
    wide = key_high.shape[1]
    grad = dot3(split(values[...]), state, NN) + totals + inner[:, :wide]
    feat = (key_high[...], key_low[...])
    grad_logits = logit_grad(joined(feat), grad)
    logit_ref[...] = grad_logits
    weights[...] = dot3(split(keys[...]), split(grad_logits), TN)
    rows = parts[0].shape[0]
    for m, target in enumerate(parts):
        target[...] = weights[pl.ds(pl.multiple_of((mine ^ m) * rows, 8), rows), :]


def key_out_body(part, logits, inner, state_high, state_low, weight, key_high, key_low, *refs):
    parts, both = refs[:-1], refs[-1]
    mine = lax.axis_index("head")
    width = weight.shape[0]
    wide = key_high.shape[1]
    feat = (key_high[...], key_low[...])
    both[:, :width] = dot3(split(logits[...]), split(weight[...]), NT)
    both[:, width:] = inner[:, wide:] + dot3(feat, (state_high[...], state_low[...]), NT)
    for m, target in enumerate(parts):
        target[...] = both[pl.ds(pl.multiple_of((mine ^ m) * part, 8), part), :]


def key_sum_body(*refs):
    pieces, (grad_key, grad_value) = refs[:-2], refs[-2:]
    total = pieces[0][...]
    for piece in pieces[1:]:
        total = total + piece[...]
    width = grad_key.shape[1]
    grad_key[...] = total[:, :width]
    grad_value[...] = total[:, width:]


def weight_message_body(*refs):
    parts, shard, message = refs[:-2], refs[-2], refs[-1]
    total = parts[0][...]
    for piece in parts[1:]:
        total = total + piece[...]
    rows = total.shape[0]
    message[0:rows] = total
    message[rows:] = shard[...]


def weight_share_body(rows, *refs):
    pieces, share = refs[:-1], refs[-1]
    total = pieces[0][0:rows]
    for piece in pieces[1:]:
        total = total + piece[0:rows]
    share[...] = total


def weight_gather_body(now, rows, *refs):
    pieces, gathered = refs[:-1], refs[-1]
    mine = position(now)
    shard = pieces[0].shape[0] - rows
    for m, piece in enumerate(pieces):
        at = pl.ds(pl.multiple_of((mine ^ m) * shard, 8), shard)
        gathered[at, :] = piece[rows:]


def gather_body(rows, *refs):
    pieces, result = refs[:-1], refs[-1]
    mine = lax.axis_index("head")
    for m, piece in enumerate(pieces):
        result[pl.ds(pl.multiple_of((mine ^ m) * rows, 8), rows), :] = piece[...]


def backward(queries, keys, values, cotangent, source_ids, source_weights, q_feature, k_feature):
    heads, width, half = q_feature.shape
    wide = 2 * half
    rows = queries.shape[0]
    peers = lax.axis_size("head")
    share = width // peers
    part = rows // peers
    block = min(256, rows)
    rising, rising_ups = rounds_of(lax.axis_size("ctx"), peers, True)
    falling, falling_ups = rounds_of(lax.axis_size("ctx"), peers, False)
    message = (2 * share + 8, half)
    bind = functools.partial
    unit = 2 * rows * width * wide
    hbm = pl.BlockSpec(memory_space=pltpu.HBM)

    source_index = lax.broadcasted_iota(jnp.int32, (1, source_weights.shape[0]), 1)
    lookup = source_ids[:, None] == source_index
    weight = jnp.sum(jnp.where(lookup, source_weights[None, :], 0.0), axis=1)
    scaled = cotangent * weight[:, None]

    feat_shape = out((rows, wide), BF16)
    key_high, key_low, local = call(
        bind(key_body, share),
        [feat_shape, feat_shape, out(message)],
        [pltpu.with_memory_space_constraint(x, pltpu.HBM) for x in (keys, values, k_feature)],
        6 * unit,
        [hbm] * 3,
        scratch=[
            pltpu.VMEM((width, wide), F32),
            pltpu.VMEM(keys.shape, F32),
            pltpu.VMEM(values.shape, F32),
            pltpu.VMEM(k_feature.shape, F32),
            pltpu.SemaphoreType.DMA((3,)),
        ],
    )

    def neighbor_sum(local, rounds, ups, prefix, weights=()):
        heads_now, kept = 0, None
        held, values = (), local
        for place, now in enumerate(rounds[:-1]):
            received = swap(values, now)
            after = rounds[place + 1]
            tall = message
            final = place + 2 == len(rounds)
            outs, scratch = [out(message)] * (1 if final else 2), []
            extra = ()
            if final and weights:
                heads_now = len(weights)
                shard = heads_now * width // after[2]
                outs.append(out((shard, half)))
                tall = (message[0] + shard, half)
                scratch = [pltpu.VMEM((heads_now * width, half), F32)]
                extra = tuple(weights)
            results = call(
                bind(step_body, now, after, ups, prefix, place == 0, final, heads_now),
                outs + [out(tall)] * (after[2] - 1),
                (local, *held, *received, *extra),
                scratch=scratch,
            )
            keep = 1 if final else 2
            held, results = tuple(results[:keep]), results[keep:]
            if extra:
                kept, results = results[0], results[1:]
            values = results
        received = swap(values, rounds[-1])
        (result,) = call(
            bind(last_body, rounds[-1], ups, prefix), [out(message)], (held[0], *received)
        )
        if kept is None:
            return result, None
        (shard_sum,) = call(bind(shard_sum_body, message[0]), [out(kept.shape)], (kept, *received))
        return result, shard_sum

    before, _ = neighbor_sum(local, rising, rising_ups, True)
    prefix = [before] + exchange(before, peers)

    def query_spec(h):
        return pl.BlockSpec((rows, width), lambda i: (0, h))

    feats, scores, inner = [], [], []
    for h in range(heads):
        args = (queries, q_feature, values, key_high, key_low)
        outs = (
            [feat_shape] * 2 + [out((rows, rows), BF16)] * 2 + [out((rows, width))] * 2
        )
        results = call(
            bind(query_body, block),
            outs,
            args,
            9 * unit,
            [query_spec(h), pl.BlockSpec((1, width, half), lambda i, h=h: (h, 0, 0))]
            + [whole(a.shape) for a in args[2:]],
            [whole(o.shape) for o in outs],
        )
        feats.append(results[0:2])
        scores.append(results[2:4])
        inner.append(results[4:6])

    results = call(
        bind(inter_body, heads, peers, share),
        [out((2 * width, wide), BF16)] * 2
        + [out((rows, 2 * width))] * heads
        + [out(message)] * peers,
        (
            *prefix,
            *[x for pair in feats for x in pair],
            *[x for pair in inner for x in pair],
            scaled,
        ),
        12 * heads * unit,
        scratch=[pltpu.VMEM((width, wide), F32)],
    )
    state, results = results[:2], results[2:]
    grads, results = results[:heads], results[heads:]
    sends = exchange(results[1:], peers)
    (carried,) = call(sum_body, [out(message)], (results[0], *sends))

    weight_grads, query_logits, key_inner = [], [], None
    for h in range(heads):
        args = [queries, values, key_high, key_low, *feats[h], *scores[h], grads[h], *state]
        outs = [out((rows, half)), out((width, half)), out((rows, wide + width))]
        if h > 0:
            args.append(key_inner)
        logits, grad_weight, key_inner = call(
            bind(query_grad_body, block, h == 0),
            outs,
            args,
            14 * unit,
            [query_spec(h)] + [whole(a.shape) for a in args[1:]],
            [whole(o.shape) for o in outs],
        )
        query_logits.append(logits)
        weight_grads.append(grad_weight)
    (grad_queries,) = call(
        bind(query_out_body, heads),
        [out((rows, heads * width))],
        (q_feature, *query_logits),
        3 * unit,
    )

    later, q_shard = neighbor_sum(carried, falling, falling_ups, False, weight_grads)
    shard = q_shard.shape[0]

    weight_rows = width // peers
    results = call(
        bind(key_grad_body, share),
        [out((rows, half))]
        + [out((width, wide), BF16)] * 2
        + [out((weight_rows, half))] * peers,
        (later, key_inner, values, keys, key_high, key_low),
        6 * unit,
        scratch=[pltpu.VMEM((width, wide), F32), pltpu.VMEM((width, half), F32)],
    )
    key_logits, later_high, later_low = results[:3]
    weight_parts = results[3:]
    weight_parts = [weight_parts[0]] + exchange(weight_parts[1:], peers)
    (total,) = call(
        weight_message_body, [out((weight_rows + shard, half))], (*weight_parts, q_shard)
    )
    key_parts = call(
        bind(key_out_body, part),
        [out((part, 2 * width))] * peers,
        (key_logits, key_inner, later_high, later_low, k_feature, key_high, key_low),
        6 * unit,
        scratch=[pltpu.VMEM((rows, 2 * width), F32)],
    )
    key_parts = [key_parts[0]] + exchange(key_parts[1:], peers)
    grad_keys, grad_values = call(key_sum_body, [out((part, width))] * 2, key_parts)
    for now in falling[:-1]:
        received = swap(total, now)
        (total,) = call(sum_body, [out(total.shape)], (total, *received))
    received = swap(total, falling[-1])
    (k_share,) = call(
        bind(weight_share_body, weight_rows), [out((weight_rows, half))], (total, *received)
    )
    shares = [k_share] + exchange(k_share, peers)
    (k_sum,) = call(bind(gather_body, weight_rows), [out((width, half))], shares)
    (q_sum,) = call(
        bind(weight_gather_body, falling[-1], weight_rows),
        [out((heads * width, half))],
        (total, *received),
    )
    return (
        grad_queries,
        grad_keys,
        grad_values,
        q_sum.reshape(heads, width, half),
        k_sum,
    )


def solution(mesh):
    placed = (
        P("ctx", "head"),
        P("ctx", None),
        P("ctx", None),
        P("ctx", "head"),
        P("ctx"),
        P(),
        P("head", None, None),
        P(),
    )
    return jax.shard_map(
        backward,
        mesh=mesh,
        in_specs=placed,
        out_specs=(
            P("ctx", "head"),
            P(("ctx", "head"), None),
            P(("ctx", "head"), None),
            P("head", None, None),
            P(),
        ),
        check_vma=False,
    )
```

```python
import functools

import jax
import jax.numpy as jnp
from jax import lax
from jax.experimental import pallas as pl
from jax.experimental.pallas import tpu as pltpu
from jax.sharding import PartitionSpec as P


F32 = jnp.float32
BF16 = jnp.bfloat16
NN = ((1,), (0,))
NT = ((1,), (1,))
TN = ((0,), (0,))


def split(x):
    high = x.astype(BF16)
    return high, (x - high.astype(F32)).astype(BF16)


def joined(pair):
    return pair[0].astype(F32) + pair[1].astype(F32)


def raw_dot(a, b, dims):
    return lax.dot_general(a, b, (dims, ((), ())), preferred_element_type=F32)


def dot3(a, b, dims):
    inner, outer = dims[1][0], 1 - dims[1][0]
    columns = b[0].shape[outer]
    depth = b[0].shape[inner]
    short = depth <= 128
    left = jnp.concatenate(a, axis=dims[0][0]) if short else a[0]
    doubled = jnp.concatenate([b[0], b[0]], axis=inner) if short else b[0]
    if columns <= 128:
        side = jnp.concatenate([b[1], jnp.zeros_like(b[1])], axis=inner) if short else b[1]
        first = raw_dot(left, jnp.concatenate([doubled, side], axis=outer), dims)
        rest = first[:, columns:]
    else:
        first = raw_dot(left, doubled, dims)
        rest = raw_dot(a[0], b[1], dims)
    if not short:
        rest = rest + raw_dot(a[1], b[0], dims)
    return first[:, :columns] + rest


def split3(x):
    high = x.astype(BF16)
    rest = x - high.astype(F32)
    middle = rest.astype(BF16)
    return high, middle, (rest - middle.astype(F32)).astype(BF16)


def dot_exact(a, b):
    (ah, am, al), (bh, bm, bl) = split3(a), split3(b)
    columns = b.shape[1]
    stacked = lambda x, y, axis: jnp.concatenate([x, y], axis=axis)
    square = stacked(stacked(bh, bm, 1), stacked(bm, bh, 1), 0)
    first = raw_dot(stacked(ah, am, 1), square, NN)
    rest = raw_dot(stacked(ah, al, 1), stacked(bl, bh, 0), NN)
    return first[:, :columns] + (first[:, columns:] + rest)


def softmaxes(logits):
    upper = jnp.exp(logits - jnp.max(logits, axis=-1, keepdims=True))
    lower = jnp.exp(jnp.min(logits, axis=-1, keepdims=True) - logits)
    return (
        upper / jnp.sum(upper, axis=-1, keepdims=True),
        lower / jnp.sum(lower, axis=-1, keepdims=True),
    )


def logit_grad(features, grad):
    half = features.shape[1] // 2
    upper, lower = features[:, :half], features[:, half:]
    a, b = grad[:, :half], grad[:, half:]
    up = upper * (a - jnp.sum(upper * a, axis=-1, keepdims=True))
    return up - lower * (b - jnp.sum(lower * b, axis=-1, keepdims=True))


def digits_of(count):
    found, base = [], 1
    while base < count:
        radix = 4 if (count // base) % 4 == 0 else 2
        found.append((base, radix))
        base *= radix
    return found


def rounds_of(count, peers, rising):
    digits = digits_of(count)
    radices = [radix for _, radix in digits]
    joint = peers % 2 == 0 and radices == radices[::-1]
    even = digits if rising else digits[::-1]
    odd = even[::-1] if joint else even
    ups = (rising, (not rising) if joint else rising)
    return [(e[0], o[0], e[1]) for e, o in zip(even, odd)], ups


def position(step):
    even, odd, radix = step
    index = lax.axis_index("ctx")
    is_odd = lax.axis_index("head") % 2 == 1
    return jnp.where(is_odd, (index // odd) % radix, (index // even) % radix)


def is_up(ups):
    return (lax.axis_index("head") % 2 == 1) == ups[1] if ups[0] != ups[1] else ups[0]


def swap(values, step):
    even, odd, radix = step
    count, peers = lax.axis_size("ctx"), lax.axis_size("head")
    received = []
    for m in range(1, radix):
        value = values[m - 1] if isinstance(values, (list, tuple)) else values
        pairs = [
            (i * peers + h, (i ^ (m * (odd if h % 2 else even))) * peers + h)
            for i in range(count)
            for h in range(peers)
        ]
        received.append(lax.ppermute(value, ("ctx", "head"), pairs))
    return received


def exchange(values, peers):
    received = []
    for m in range(1, peers):
        value = values[m - 1] if isinstance(values, (list, tuple)) else values
        received.append(lax.ppermute(value, "head", [(i, i ^ m) for i in range(peers)]))
    return received


def grant(size):
    return (4 << 20) + 3 * size


def call(body, outs, args, flops=0, in_specs=None, out_specs=None, scratch=()):
    size = sum(4 * a.size for a in args) + sum(4 * o.size for o in outs)
    kwargs = {}
    if in_specs is not None:
        kwargs["in_specs"] = in_specs
    if out_specs is not None:
        kwargs["out_specs"] = out_specs
        kwargs["grid"] = (1,)
    return pl.pallas_call(
        body,
        out_shape=outs,
        scratch_shapes=scratch,
        cost_estimate=pl.CostEstimate(flops=flops, bytes_accessed=size, transcendentals=0),
        compiler_params=pltpu.CompilerParams(vmem_limit_bytes=grant(size)),
        **kwargs,
    )(*args)


def whole(shape):
    return pl.BlockSpec(shape, lambda i: (0,) * len(shape))


def out(shape, dtype=F32):
    return jax.ShapeDtypeStruct(shape, dtype)


def put_rows(ref, state):
    rows, half = state.shape[0], state.shape[1] // 2
    ref[0:rows] = state[:, :half]
    ref[rows : 2 * rows] = state[:, half:]


def totals_block(totals):
    half = totals.shape[1] // 2
    first = lax.broadcasted_iota(jnp.int32, (8, half), 0) < 4
    return jnp.where(first, totals[:, :half], totals[:, half:])


def take_totals(piece, rows):
    return jnp.concatenate(
        [piece[2 * rows : 2 * rows + 1], piece[2 * rows + 4 : 2 * rows + 5]], axis=1
    )


def put_state(piece, scratch, rows, owner):
    half = piece.shape[1]
    at = pl.ds(pl.multiple_of(owner * rows, 8), rows)
    scratch[at, :half] = piece[0:rows]
    scratch[at, half:] = piece[rows : 2 * rows]


def key_body(
    share, keys_hbm, values_hbm, weight_hbm, feat_high, feat_low, message,
    scratch, keys, values, weight, arrived,
):
    mine = lax.axis_index("head")
    pairs = [(keys_hbm, keys), (weight_hbm, weight), (values_hbm, values)]
    copies = [
        pltpu.make_async_copy(source, target, arrived.at[n])
        for n, (source, target) in enumerate(pairs)
    ]
    for copy in copies:
        copy.start()
    copies[0].wait()
    copies[1].wait()
    upper, lower = softmaxes(dot_exact(keys[...], weight[...]))
    feat = split(jnp.concatenate([upper, lower], axis=1))
    feat_high[...] = feat[0]
    feat_low[...] = feat[1]
    ones = jnp.ones((8, feat[0].shape[0]), BF16)
    totals = raw_dot(ones, feat[0], NN) + raw_dot(ones, feat[1], NN)
    copies[2].wait()
    scratch[...] = dot3(split(values[...]), feat, TN)
    state = scratch[pl.ds(pl.multiple_of(mine * share, 8), share), :]
    put_rows(message, state)
    message[2 * share :] = totals_block(totals)


def causal(size):
    row = lax.broadcasted_iota(jnp.int32, (size, size), 0)
    col = lax.broadcasted_iota(jnp.int32, (size, size), 1)
    return row >= col


def query_body(
    block, queries, weight, values, key_high, key_low,
    feat_high, feat_low, score_high, score_low, numer, norm,
):
    upper, lower = softmaxes(dot_exact(queries[...], weight[0]))
    feat = split(jnp.concatenate([upper, lower], axis=1))
    feat_high[...] = feat[0]
    feat_low[...] = feat[1]
    rows, width = values.shape
    extended = split(jnp.concatenate([values[...], jnp.ones((rows, width), F32)], axis=1))
    mask = causal(block)
    for i in range(rows // block):
        at = slice(i * block, (i + 1) * block)
        total = None
        for j in range(i + 1):
            past = slice(j * block, (j + 1) * block)
            scores = dot3((feat[0][at], feat[1][at]), (key_high[past], key_low[past]), NT)
            if i == j:
                scores = jnp.where(mask, scores, 0.0)
            pair = split(scores)
            score_high[at, past] = pair[0]
            score_low[at, past] = pair[1]
            term = dot3(pair, (extended[0][past], extended[1][past]), NN)
            total = term if total is None else total + term
        numer[at] = total[:, :width]
        norm[at] = total[:, width:]


def counts(prefix, mine, m):
    return (mine ^ m) < mine if prefix else (mine ^ m) > mine


def step_body(now, after, ups, prefix, first, final, heads, local, *refs):
    held, refs = ([], refs) if first else (refs[:2], refs[2:])
    received, refs = refs[: now[2] - 1], refs[now[2] - 1 :]
    weights, refs = refs[:heads], refs[heads:]
    up, mine, then = is_up(ups), position(now), position(after)
    own = local[...]
    size = own.shape[0]
    total = own if first else held[1][...]
    part = jnp.zeros(own.shape, F32) if first else held[0][...]
    for m, piece in enumerate(received, 1):
        value = piece[...]
        total = total + value
        take = counts(prefix, mine, m)
        if not first:
            take = jnp.logical_or(take, jnp.logical_not(up))
        part = part + jnp.where(take, value, 0.0)
    refs[0][...] = part
    if not final:
        refs[1][...] = total
    refs = refs[1 if final else 2 :]
    if heads:
        scratch, kept, refs = refs[-1], refs[0], refs[1:-1]
        width = weights[0].shape[0]
        shard = kept.shape[0]
        for h, weight in enumerate(weights):
            scratch[h * width : (h + 1) * width] = weight[...]
        rows = lambda m: pl.ds(pl.multiple_of((then ^ m) * shard, 8), shard)
        kept[...] = scratch[rows(0), :]
    for m, message in enumerate(refs, 1):
        falling = part + jnp.where(counts(prefix, then, m), 0.0, own)
        message[0:size] = jnp.where(up, total, falling)
        if heads:
            message[size:] = scratch[rows(m), :]


def last_body(now, ups, prefix, part, *refs):
    received, refs = refs[: now[2] - 1], refs[now[2] - 1 :]
    up, mine = is_up(ups), position(now)
    total = part[...]
    size = total.shape[0]
    for m, piece in enumerate(received, 1):
        take = jnp.logical_or(counts(prefix, mine, m), jnp.logical_not(up))
        total = total + jnp.where(take, piece[0:size], 0.0)
    refs[-1][...] = total


def shard_sum_body(size, kept, *refs):
    total = kept[...]
    for piece in refs[:-1]:
        total = total + piece[size:]
    refs[-1][...] = total


def carried_body(heads, share, before, scaled, *refs):
    feats, refs = [refs[2 * h : 2 * h + 2] for h in range(heads)], refs[2 * heads :]
    locals_, refs = refs[:heads], refs[heads:]
    norms, refs = refs[:heads], refs[heads:]
    grads, refs = refs[:heads], refs[heads:]
    messages, scratch = refs[:-1], refs[-1]
    mine = lax.axis_index("head")
    width = grads[0].shape[1]
    totals = take_totals(before, share)
    totals = split(jnp.broadcast_to(totals, (width, totals.shape[1])))
    carried = None
    for h in range(heads):
        feat = (feats[h][0][...], feats[h][1][...])
        norm = locals_[h][...] + dot3(feat, totals, NT)
        norms[h][...] = norm
        grad_numer = scaled[:, h * width : (h + 1) * width] / norm
        grads[h][...] = grad_numer
        term = dot3(split(grad_numer), feat, TN)
        carried = term if carried is None else carried + term
    scratch[...] = carried
    for m, message in enumerate(messages):
        put_rows(message, scratch[pl.ds(pl.multiple_of((mine ^ m) * share, 8), share), :])


def inter_body(heads, peers, share, scaled, *refs):
    pieces, refs = refs[:peers], refs[peers:]
    feats, refs = [refs[2 * h : 2 * h + 2] for h in range(heads)], refs[2 * heads :]
    locals_, refs = refs[:heads], refs[heads:]
    norms, refs = refs[:heads], refs[heads:]
    state_high, state_low, carried_totals, *refs = refs
    grads, scratch = refs[:heads], refs[-1]
    mine = lax.axis_index("head")
    for m, piece in enumerate(pieces):
        put_state(piece, scratch, share, mine ^ m)
    state = scratch[...]
    width = state.shape[0]
    totals = jnp.broadcast_to(take_totals(pieces[0], share), state.shape)
    pair = split(state)
    state_high[:width] = pair[0]
    state_low[:width] = pair[1]
    rest = split(totals)
    state_high[width:] = rest[0]
    state_low[width:] = rest[1]
    carried = None
    for h in range(heads):
        feat = (feats[h][0][...], feats[h][1][...])
        numer = locals_[h][...] + dot3(feat, pair, NT)
        norm = norms[h][...]
        mine_scaled = scaled[:, h * width : (h + 1) * width]
        along = jnp.sum(mine_scaled * (numer / norm), axis=1, keepdims=True)
        grad_norm = -(along / norm)
        grads[h][...] = grad_norm
        wide_norm = jnp.concatenate([grad_norm, grad_norm], axis=1)
        term = jnp.sum(wide_norm * joined(feat), axis=0, keepdims=True)
        carried = term if carried is None else carried + term
    carried_totals[...] = totals_block(jnp.broadcast_to(carried, (8, carried.shape[1])))


def carried_sum_body(totals, *refs):
    total = refs[0][...]
    for piece in refs[1:-1]:
        total = total + piece[...]
    rows = total.shape[0]
    refs[-1][0:rows] = total
    refs[-1][rows:] = totals[...]


def cut(pair, at):
    return pair[0][at], pair[1][at]


def query_grad_body(
    block, queries, values, key_high, key_low, feat_high, feat_low, grad_numer, grad_norm,
    state_high, state_low, logit_ref, grad_weight, score_grad_high, score_grad_low,
):
    rows, width = values.shape
    numer = split(grad_numer[...])
    norm_grad = grad_norm[...]
    scaled_norm = split(norm_grad * (1.0 / width))
    extended = [jnp.concatenate([a, b], axis=1) for a, b in zip(numer, scaled_norm)]
    value_pair = split(values[...])
    feat = (feat_high[...], feat_low[...])
    state = (state_high[...], state_low[...])
    mask = causal(block)
    parts = []
    for i in range(rows // block):
        at = slice(i * block, (i + 1) * block)
        norm_part = jnp.concatenate([norm_grad[at]] * (block // width), axis=1)
        grad_query = dot3(cut(extended, at), state, NN)
        for j in range(i + 1):
            past = slice(j * block, (j + 1) * block)
            grad_scores = dot3(cut(numer, at), cut(value_pair, past), NT) + norm_part
            if i == j:
                grad_scores = jnp.where(mask, grad_scores, 0.0)
            pair = split(grad_scores)
            score_grad_high[at, past] = pair[0]
            score_grad_low[at, past] = pair[1]
            grad_query = grad_query + dot3(pair, (key_high[past], key_low[past]), NN)
        parts.append(logit_grad(joined(cut(feat, at)), grad_query))
    grad_logits = jnp.concatenate(parts, axis=0)
    logit_ref[...] = grad_logits
    grad_weight[...] = dot3(split(queries[...]), split(grad_logits), TN)


def key_inner_body(block, heads, *refs):
    result = refs[-1]
    rows, wide = refs[0].shape
    count = rows // block
    key_sums, value_sums = [None] * count, [None] * count
    for h in range(heads):
        *pairs, grads = refs[7 * h : 7 * h + 7]
        feat, scores, score_grads = pairs[0:2], pairs[2:4], pairs[4:6]
        numer = split(grads[...])
        for i in range(count):
            at = slice(i * block, (i + 1) * block)
            for j in range(i + 1):
                past = slice(j * block, (j + 1) * block)
                pair = (score_grads[0][at, past], score_grads[1][at, past])
                term = dot3(pair, cut(feat, at), TN)
                key_sums[j] = term if key_sums[j] is None else key_sums[j] + term
                pair = (scores[0][at, past], scores[1][at, past])
                term = dot3(pair, cut(numer, at), TN)
                value_sums[j] = term if value_sums[j] is None else value_sums[j] + term
    for j in range(count):
        past = slice(j * block, (j + 1) * block)
        result[past, :wide] = key_sums[j]
        result[past, wide:] = value_sums[j]


def query_out_body(heads, weights, *refs):
    logits, result = refs[:heads], refs[heads]
    width = weights.shape[1]
    for h in range(heads):
        result[:, h * width : (h + 1) * width] = dot3(
            split(logits[h][...]), split(weights[h]), NT
        )


def sum_body(*refs):
    total = refs[0][...]
    for piece in refs[1:-1]:
        total = total + piece[...]
    refs[-1][...] = total


def key_grad_body(share, piece, inner, values, keys, key_high, key_low, *refs):
    logit_ref, state_high, state_low, *parts, scratch, weights = refs
    mine = lax.axis_index("head")
    scratch[...] = jnp.zeros(scratch.shape, F32)
    put_state(piece, scratch, share, mine)
    state = split(scratch[...])
    state_high[...] = state[0]
    state_low[...] = state[1]
    totals = take_totals(piece, share)
    wide = key_high.shape[1]
    grad = dot3(split(values[...]), state, NN) + totals + inner[:, :wide]
    feat = (key_high[...], key_low[...])
    grad_logits = logit_grad(joined(feat), grad)
    logit_ref[...] = grad_logits
    weights[...] = dot3(split(keys[...]), split(grad_logits), TN)
    rows = parts[0].shape[0]
    for m, target in enumerate(parts):
        target[...] = weights[pl.ds(pl.multiple_of((mine ^ m) * rows, 8), rows), :]


def key_out_body(part, logits, inner, state_high, state_low, weight, key_high, key_low, *refs):
    parts, both = refs[:-1], refs[-1]
    mine = lax.axis_index("head")
    width = weight.shape[0]
    wide = key_high.shape[1]
    feat = (key_high[...], key_low[...])
    both[:, :width] = dot3(split(logits[...]), split(weight[...]), NT)
    both[:, width:] = inner[:, wide:] + dot3(feat, (state_high[...], state_low[...]), NT)
    for m, target in enumerate(parts):
        target[...] = both[pl.ds(pl.multiple_of((mine ^ m) * part, 8), part), :]


def key_sum_body(*refs):
    pieces, (grad_key, grad_value) = refs[:-2], refs[-2:]
    total = pieces[0][...]
    for piece in pieces[1:]:
        total = total + piece[...]
    width = grad_key.shape[1]
    grad_key[...] = total[:, :width]
    grad_value[...] = total[:, width:]


def weight_message_body(*refs):
    parts, shard, message = refs[:-2], refs[-2], refs[-1]
    total = parts[0][...]
    for piece in parts[1:]:
        total = total + piece[...]
    rows = total.shape[0]
    message[0:rows] = total
    message[rows:] = shard[...]


def weight_share_body(rows, *refs):
    pieces, share = refs[:-1], refs[-1]
    total = pieces[0][0:rows]
    for piece in pieces[1:]:
        total = total + piece[0:rows]
    share[...] = total


def weight_gather_body(now, rows, *refs):
    pieces, gathered = refs[:-1], refs[-1]
    mine = position(now)
    shard = pieces[0].shape[0] - rows
    for m, piece in enumerate(pieces):
        at = pl.ds(pl.multiple_of((mine ^ m) * shard, 8), shard)
        gathered[at, :] = piece[rows:]


def gather_body(rows, *refs):
    pieces, result = refs[:-1], refs[-1]
    mine = lax.axis_index("head")
    for m, piece in enumerate(pieces):
        result[pl.ds(pl.multiple_of((mine ^ m) * rows, 8), rows), :] = piece[...]


def backward(queries, keys, values, cotangent, source_ids, source_weights, q_feature, k_feature):
    heads, width, half = q_feature.shape
    wide = 2 * half
    rows = queries.shape[0]
    peers = lax.axis_size("head")
    share = width // peers
    part = rows // peers
    block = min(256, rows)
    rising, rising_ups = rounds_of(lax.axis_size("ctx"), peers, True)
    falling, falling_ups = rounds_of(lax.axis_size("ctx"), peers, False)
    message = (2 * share + 8, half)
    bind = functools.partial
    unit = 2 * rows * width * wide
    hbm = pl.BlockSpec(memory_space=pltpu.HBM)

    source_index = lax.broadcasted_iota(jnp.int32, (1, source_weights.shape[0]), 1)
    lookup = source_ids[:, None] == source_index
    weight = jnp.sum(jnp.where(lookup, source_weights[None, :], 0.0), axis=1)
    scaled = cotangent * weight[:, None]

    feat_shape = out((rows, wide), BF16)
    key_high, key_low, local = call(
        bind(key_body, share),
        [feat_shape, feat_shape, out(message)],
        [pltpu.with_memory_space_constraint(x, pltpu.HBM) for x in (keys, values, k_feature)],
        6 * unit,
        [hbm] * 3,
        scratch=[
            pltpu.VMEM((width, wide), F32),
            pltpu.VMEM(keys.shape, F32),
            pltpu.VMEM(values.shape, F32),
            pltpu.VMEM(k_feature.shape, F32),
            pltpu.SemaphoreType.DMA((3,)),
        ],
    )

    def neighbor_sum(local, rounds, ups, prefix, weights=()):
        heads_now, kept = 0, None
        held, values = (), local
        for place, now in enumerate(rounds[:-1]):
            received = swap(values, now)
            after = rounds[place + 1]
            tall = message
            final = place + 2 == len(rounds)
            outs, scratch = [out(message)] * (1 if final else 2), []
            extra = ()
            if final and weights:
                heads_now = len(weights)
                shard = heads_now * width // after[2]
                outs.append(out((shard, half)))
                tall = (message[0] + shard, half)
                scratch = [pltpu.VMEM((heads_now * width, half), F32)]
                extra = tuple(weights)
            results = call(
                bind(step_body, now, after, ups, prefix, place == 0, final, heads_now),
                outs + [out(tall)] * (after[2] - 1),
                (local, *held, *received, *extra),
                scratch=scratch,
            )
            keep = 1 if final else 2
            held, results = tuple(results[:keep]), results[keep:]
            if extra:
                kept, results = results[0], results[1:]
            values = results
        received = swap(values, rounds[-1])
        (result,) = call(
            bind(last_body, rounds[-1], ups, prefix), [out(message)], (held[0], *received)
        )
        if kept is None:
            return result, None
        (shard_sum,) = call(bind(shard_sum_body, message[0]), [out(kept.shape)], (kept, *received))
        return result, shard_sum

    before, _ = neighbor_sum(local, rising, rising_ups, True)
    prefix = [before] + exchange(before, peers)

    def query_spec(h):
        return pl.BlockSpec((rows, width), lambda i: (0, h))

    feats, scores, inner = [], [], []
    for h in range(heads):
        args = (queries, q_feature, values, key_high, key_low)
        outs = (
            [feat_shape] * 2 + [out((rows, rows), BF16)] * 2 + [out((rows, width))] * 2
        )
        results = call(
            bind(query_body, block),
            outs,
            args,
            9 * unit,
            [query_spec(h), pl.BlockSpec((1, width, half), lambda i, h=h: (h, 0, 0))]
            + [whole(a.shape) for a in args[2:]],
            [whole(o.shape) for o in outs],
        )
        feats.append(results[0:2])
        scores.append(results[2:4])
        inner.append(results[4:6])

    flat_feats = [x for pair in feats for x in pair]
    results = call(
        bind(carried_body, heads, share),
        [out((rows, width))] * (2 * heads) + [out((2 * share, half))] * peers,
        (before, scaled, *flat_feats, *[pair[1] for pair in inner]),
        6 * heads * unit,
        scratch=[pltpu.VMEM((width, wide), F32)],
    )
    norms, results = results[:heads], results[heads:]
    grads, results = results[:heads], results[heads:]
    carried_parts = [results[0]] + exchange(results[1:], peers)
    results = call(
        bind(inter_body, heads, peers, share),
        [out((2 * width, wide), BF16)] * 2
        + [out((8, half))]
        + [out((rows, width))] * heads,
        (scaled, *prefix, *flat_feats, *[pair[0] for pair in inner], *norms),
        4 * heads * unit,
        scratch=[pltpu.VMEM((width, wide), F32)],
    )
    state, carried_totals, norm_grads = results[:2], results[2], results[3:]
    (carried,) = call(carried_sum_body, [out(message)], (carried_totals, *carried_parts))

    weight_grads, query_logits, inner_args = [], [], []
    for h in range(heads):
        args = [
            queries, values, key_high, key_low, *feats[h], grads[h], norm_grads[h], *state,
        ]
        outs = [out((rows, half)), out((width, half))] + [out((rows, rows), BF16)] * 2
        logits, grad_weight, *score_grads = call(
            bind(query_grad_body, block),
            outs,
            args,
            8 * unit,
            [query_spec(h)] + [whole(a.shape) for a in args[1:]],
            [whole(o.shape) for o in outs],
        )
        query_logits.append(logits)
        weight_grads.append(grad_weight)
        inner_args += [*feats[h], *scores[h], *score_grads, grads[h]]
    (key_inner,) = call(
        bind(key_inner_body, block, heads),
        [out((rows, wide + width))],
        inner_args,
        6 * heads * unit,
    )
    (grad_queries,) = call(
        bind(query_out_body, heads),
        [out((rows, heads * width))],
        (q_feature, *query_logits),
        3 * unit,
    )

    later, q_shard = neighbor_sum(carried, falling, falling_ups, False, weight_grads)
    shard = q_shard.shape[0]

    weight_rows = width // peers
    results = call(
        bind(key_grad_body, share),
        [out((rows, half))]
        + [out((width, wide), BF16)] * 2
        + [out((weight_rows, half))] * peers,
        (later, key_inner, values, keys, key_high, key_low),
        6 * unit,
        scratch=[pltpu.VMEM((width, wide), F32), pltpu.VMEM((width, half), F32)],
    )
    key_logits, later_high, later_low = results[:3]
    weight_parts = results[3:]
    weight_parts = [weight_parts[0]] + exchange(weight_parts[1:], peers)
    (total,) = call(
        weight_message_body, [out((weight_rows + shard, half))], (*weight_parts, q_shard)
    )
    key_parts = call(
        bind(key_out_body, part),
        [out((part, 2 * width))] * peers,
        (key_logits, key_inner, later_high, later_low, k_feature, key_high, key_low),
        6 * unit,
        scratch=[pltpu.VMEM((rows, 2 * width), F32)],
    )
    key_parts = [key_parts[0]] + exchange(key_parts[1:], peers)
    grad_keys, grad_values = call(key_sum_body, [out((part, width))] * 2, key_parts)
    for now in falling[:-1]:
        received = swap(total, now)
        (total,) = call(sum_body, [out(total.shape)], (total, *received))
    received = swap(total, falling[-1])
    (k_share,) = call(
        bind(weight_share_body, weight_rows), [out((weight_rows, half))], (total, *received)
    )
    shares = [k_share] + exchange(k_share, peers)
    (k_sum,) = call(bind(gather_body, weight_rows), [out((width, half))], shares)
    (q_sum,) = call(
        bind(weight_gather_body, falling[-1], weight_rows),
        [out((heads * width, half))],
        (total, *received),
    )
    return (
        grad_queries,
        grad_keys,
        grad_values,
        q_sum.reshape(heads, width, half),
        k_sum,
    )


def solution(mesh):
    placed = (
        P("ctx", "head"),
        P("ctx", None),
        P("ctx", None),
        P("ctx", "head"),
        P("ctx"),
        P(),
        P("head", None, None),
        P(),
    )
    return jax.shard_map(
        backward,
        mesh=mesh,
        in_specs=placed,
        out_specs=(
            P("ctx", "head"),
            P(("ctx", "head"), None),
            P(("ctx", "head"), None),
            P("head", None, None),
            P(),
        ),
        check_vma=False,
    )
```

```python
import functools

import jax
import jax.numpy as jnp
from jax import lax
from jax.experimental import pallas as pl
from jax.experimental.pallas import tpu as pltpu
from jax.sharding import PartitionSpec as P


F32 = jnp.float32
BF16 = jnp.bfloat16
NN = ((1,), (0,))
NT = ((1,), (1,))
TN = ((0,), (0,))


def split(x):
    high = x.astype(BF16)
    return high, (x - high.astype(F32)).astype(BF16)


def joined(pair):
    return pair[0].astype(F32) + pair[1].astype(F32)


def raw_dot(a, b, dims):
    return lax.dot_general(a, b, (dims, ((), ())), preferred_element_type=F32)


def dot3(a, b, dims):
    inner, outer = dims[1][0], 1 - dims[1][0]
    columns = b[0].shape[outer]
    depth = b[0].shape[inner]
    short = depth <= 128
    left = jnp.concatenate(a, axis=dims[0][0]) if short else a[0]
    doubled = jnp.concatenate([b[0], b[0]], axis=inner) if short else b[0]
    if columns <= 128:
        side = jnp.concatenate([b[1], jnp.zeros_like(b[1])], axis=inner) if short else b[1]
        first = raw_dot(left, jnp.concatenate([doubled, side], axis=outer), dims)
        rest = first[:, columns:]
    else:
        first = raw_dot(left, doubled, dims)
        rest = raw_dot(a[0], b[1], dims)
    if not short:
        rest = rest + raw_dot(a[1], b[0], dims)
    return first[:, :columns] + rest


def dot5(a, b, dims):
    small = raw_dot(a[1], b[1], dims) + raw_dot(a[0], b[2], dims)
    return dot3(a, b[:2], dims) + small


def split3(x):
    high = x.astype(BF16)
    rest = x - high.astype(F32)
    middle = rest.astype(BF16)
    return high, middle, (rest - middle.astype(F32)).astype(BF16)


def dot_exact(a, b):
    (ah, am, al), (bh, bm, bl) = split3(a), split3(b)
    columns = b.shape[1]
    stacked = lambda x, y, axis: jnp.concatenate([x, y], axis=axis)
    square = stacked(stacked(bh, bm, 1), stacked(bm, bh, 1), 0)
    first = raw_dot(stacked(ah, am, 1), square, NN)
    rest = raw_dot(stacked(ah, al, 1), stacked(bl, bh, 0), NN)
    return first[:, :columns] + (first[:, columns:] + rest)


def softmaxes(logits):
    upper = jnp.exp(logits - jnp.max(logits, axis=-1, keepdims=True))
    lower = jnp.exp(jnp.min(logits, axis=-1, keepdims=True) - logits)
    return (
        upper / jnp.sum(upper, axis=-1, keepdims=True),
        lower / jnp.sum(lower, axis=-1, keepdims=True),
    )


def logit_grad(features, grad):
    half = features.shape[1] // 2
    upper, lower = features[:, :half], features[:, half:]
    a, b = grad[:, :half], grad[:, half:]
    up = upper * (a - jnp.sum(upper * a, axis=-1, keepdims=True))
    return up - lower * (b - jnp.sum(lower * b, axis=-1, keepdims=True))


def digits_of(count):
    found, base = [], 1
    while base < count:
        radix = 4 if (count // base) % 4 == 0 else 2
        found.append((base, radix))
        base *= radix
    return found


def rounds_of(count, peers, rising):
    digits = digits_of(count)
    radices = [radix for _, radix in digits]
    joint = peers % 2 == 0 and radices == radices[::-1]
    even = digits if rising else digits[::-1]
    odd = even[::-1] if joint else even
    ups = (rising, (not rising) if joint else rising)
    return [(e[0], o[0], e[1]) for e, o in zip(even, odd)], ups


def position(step):
    even, odd, radix = step
    index = lax.axis_index("ctx")
    is_odd = lax.axis_index("head") % 2 == 1
    return jnp.where(is_odd, (index // odd) % radix, (index // even) % radix)


def is_up(ups):
    return (lax.axis_index("head") % 2 == 1) == ups[1] if ups[0] != ups[1] else ups[0]


def swap(values, step):
    even, odd, radix = step
    count, peers = lax.axis_size("ctx"), lax.axis_size("head")
    received = []
    for m in range(1, radix):
        value = values[m - 1] if isinstance(values, (list, tuple)) else values
        pairs = [
            (i * peers + h, (i ^ (m * (odd if h % 2 else even))) * peers + h)
            for i in range(count)
            for h in range(peers)
        ]
        received.append(lax.ppermute(value, ("ctx", "head"), pairs))
    return received


def exchange(values, peers):
    received = []
    for m in range(1, peers):
        value = values[m - 1] if isinstance(values, (list, tuple)) else values
        received.append(lax.ppermute(value, "head", [(i, i ^ m) for i in range(peers)]))
    return received


def grant(size):
    return (4 << 20) + 3 * size


def call(body, outs, args, flops=0, in_specs=None, out_specs=None, scratch=()):
    size = sum(4 * a.size for a in args) + sum(4 * o.size for o in outs)
    kwargs = {}
    if in_specs is not None:
        kwargs["in_specs"] = in_specs
    if out_specs is not None:
        kwargs["out_specs"] = out_specs
        kwargs["grid"] = (1,)
    return pl.pallas_call(
        body,
        out_shape=outs,
        scratch_shapes=scratch,
        cost_estimate=pl.CostEstimate(flops=flops, bytes_accessed=size, transcendentals=0),
        compiler_params=pltpu.CompilerParams(vmem_limit_bytes=grant(size)),
        **kwargs,
    )(*args)


def whole(shape):
    return pl.BlockSpec(shape, lambda i: (0,) * len(shape))


def out(shape, dtype=F32):
    return jax.ShapeDtypeStruct(shape, dtype)


def put_rows(ref, state):
    rows, half = state.shape[0], state.shape[1] // 2
    ref[0:rows] = state[:, :half]
    ref[rows : 2 * rows] = state[:, half:]


def totals_block(totals):
    half = totals.shape[1] // 2
    first = lax.broadcasted_iota(jnp.int32, (8, half), 0) < 4
    return jnp.where(first, totals[:, :half], totals[:, half:])


def take_totals(piece, rows):
    return jnp.concatenate(
        [piece[2 * rows : 2 * rows + 1], piece[2 * rows + 4 : 2 * rows + 5]], axis=1
    )


def put_state(piece, scratch, rows, owner):
    half = piece.shape[1]
    at = pl.ds(pl.multiple_of(owner * rows, 8), rows)
    scratch[at, :half] = piece[0:rows]
    scratch[at, half:] = piece[rows : 2 * rows]


def key_body(
    share, keys_hbm, values_hbm, weight_hbm, feat_high, feat_low, feat_rest,
    message, scratch, keys, values, weight, arrived,
):
    mine = lax.axis_index("head")
    pairs = [(keys_hbm, keys), (weight_hbm, weight), (values_hbm, values)]
    copies = [
        pltpu.make_async_copy(source, target, arrived.at[n])
        for n, (source, target) in enumerate(pairs)
    ]
    for copy in copies:
        copy.start()
    copies[0].wait()
    copies[1].wait()
    upper, lower = softmaxes(dot_exact(keys[...], weight[...]))
    feat = split3(jnp.concatenate([upper, lower], axis=1))
    feat_rest[...] = feat[2]
    feat = feat[:2]
    feat_high[...] = feat[0]
    feat_low[...] = feat[1]
    ones = jnp.ones((8, feat[0].shape[0]), BF16)
    totals = raw_dot(ones, feat[0], NN) + raw_dot(ones, feat[1], NN)
    copies[2].wait()
    scratch[...] = dot3(split(values[...]), feat, TN)
    state = scratch[pl.ds(pl.multiple_of(mine * share, 8), share), :]
    put_rows(message, state)
    message[2 * share :] = totals_block(totals)


def causal(size):
    row = lax.broadcasted_iota(jnp.int32, (size, size), 0)
    col = lax.broadcasted_iota(jnp.int32, (size, size), 1)
    return row >= col


def query_body(
    block, queries, weight, values, key_high, key_low,
    feat_high, feat_low, score_high, score_low, numer, norm,
):
    upper, lower = softmaxes(dot_exact(queries[...], weight[0]))
    feat = split(jnp.concatenate([upper, lower], axis=1))
    feat_high[...] = feat[0]
    feat_low[...] = feat[1]
    rows, width = values.shape
    extended = split(jnp.concatenate([values[...], jnp.ones((rows, width), F32)], axis=1))
    mask = causal(block)
    for i in range(rows // block):
        at = slice(i * block, (i + 1) * block)
        total = None
        for j in range(i + 1):
            past = slice(j * block, (j + 1) * block)
            scores = dot3((feat[0][at], feat[1][at]), (key_high[past], key_low[past]), NT)
            if i == j:
                scores = jnp.where(mask, scores, 0.0)
            pair = split(scores)
            score_high[at, past] = pair[0]
            score_low[at, past] = pair[1]
            term = dot3(pair, (extended[0][past], extended[1][past]), NN)
            total = term if total is None else total + term
        numer[at] = total[:, :width]
        norm[at] = total[:, width:]


def counts(prefix, mine, m):
    return (mine ^ m) < mine if prefix else (mine ^ m) > mine


def step_body(now, after, ups, prefix, first, final, heads, local, *refs):
    held, refs = ([], refs) if first else (refs[:2], refs[2:])
    received, refs = refs[: now[2] - 1], refs[now[2] - 1 :]
    weights, refs = refs[:heads], refs[heads:]
    up, mine, then = is_up(ups), position(now), position(after)
    own = local[...]
    size = own.shape[0]
    total = own if first else held[1][...]
    part = jnp.zeros(own.shape, F32) if first else held[0][...]
    for m, piece in enumerate(received, 1):
        value = piece[...]
        total = total + value
        take = counts(prefix, mine, m)
        if not first:
            take = jnp.logical_or(take, jnp.logical_not(up))
        part = part + jnp.where(take, value, 0.0)
    refs[0][...] = part
    if not final:
        refs[1][...] = total
    refs = refs[1 if final else 2 :]
    if heads:
        scratch, kept, refs = refs[-1], refs[0], refs[1:-1]
        width = weights[0].shape[0]
        shard = kept.shape[0]
        for h, weight in enumerate(weights):
            scratch[h * width : (h + 1) * width] = weight[...]
        rows = lambda m: pl.ds(pl.multiple_of((then ^ m) * shard, 8), shard)
        kept[...] = scratch[rows(0), :]
    for m, message in enumerate(refs, 1):
        falling = part + jnp.where(counts(prefix, then, m), 0.0, own)
        message[0:size] = jnp.where(up, total, falling)
        if heads:
            message[size:] = scratch[rows(m), :]


def last_body(now, ups, prefix, part, *refs):
    received, refs = refs[: now[2] - 1], refs[now[2] - 1 :]
    up, mine = is_up(ups), position(now)
    total = part[...]
    size = total.shape[0]
    for m, piece in enumerate(received, 1):
        take = jnp.logical_or(counts(prefix, mine, m), jnp.logical_not(up))
        total = total + jnp.where(take, piece[0:size], 0.0)
    refs[-1][...] = total


def shard_sum_body(size, kept, *refs):
    total = kept[...]
    for piece in refs[:-1]:
        total = total + piece[size:]
    refs[-1][...] = total


def carried_body(heads, share, before, scaled, *refs):
    feats, refs = [refs[2 * h : 2 * h + 2] for h in range(heads)], refs[2 * heads :]
    locals_, refs = refs[:heads], refs[heads:]
    norms, refs = refs[:heads], refs[heads:]
    grads, refs = refs[:heads], refs[heads:]
    messages, scratch = refs[:-1], refs[-1]
    mine = lax.axis_index("head")
    width = grads[0].shape[1]
    totals = take_totals(before, share)
    totals = split(jnp.broadcast_to(totals, (width, totals.shape[1])))
    carried = None
    for h in range(heads):
        feat = (feats[h][0][...], feats[h][1][...])
        norm = locals_[h][...] + dot3(feat, totals, NT)
        norms[h][...] = norm
        grad_numer = scaled[:, h * width : (h + 1) * width] / norm
        grads[h][...] = grad_numer
        term = dot3(split(grad_numer), feat, TN)
        carried = term if carried is None else carried + term
    scratch[...] = carried
    for m, message in enumerate(messages):
        put_rows(message, scratch[pl.ds(pl.multiple_of((mine ^ m) * share, 8), share), :])


def inter_body(heads, peers, share, scaled, *refs):
    pieces, refs = refs[:peers], refs[peers:]
    feats, refs = [refs[2 * h : 2 * h + 2] for h in range(heads)], refs[2 * heads :]
    locals_, refs = refs[:heads], refs[heads:]
    norms, refs = refs[:heads], refs[heads:]
    state_high, state_low, state_rest, carried_totals, *refs = refs
    grads, scratch = refs[:heads], refs[-1]
    mine = lax.axis_index("head")
    for m, piece in enumerate(pieces):
        put_state(piece, scratch, share, mine ^ m)
    state = scratch[...]
    width = state.shape[0]
    totals = jnp.broadcast_to(take_totals(pieces[0], share), state.shape)
    parts = split3(jnp.concatenate([state, totals], axis=0))
    for target, value in zip((state_high, state_low, state_rest), parts):
        target[...] = value
    pair = (parts[0][:width], parts[1][:width])
    carried = None
    for h in range(heads):
        feat = (feats[h][0][...], feats[h][1][...])
        numer = locals_[h][...] + dot3(feat, pair, NT)
        norm = norms[h][...]
        mine_scaled = scaled[:, h * width : (h + 1) * width]
        along = jnp.sum(mine_scaled * (numer / norm), axis=1, keepdims=True)
        grad_norm = -(along / norm)
        grads[h][...] = grad_norm
        wide_norm = jnp.concatenate([grad_norm, grad_norm], axis=1)
        term = jnp.sum(wide_norm * joined(feat), axis=0, keepdims=True)
        carried = term if carried is None else carried + term
    carried_totals[...] = totals_block(jnp.broadcast_to(carried, (8, carried.shape[1])))


def carried_sum_body(totals, *refs):
    total = refs[0][...]
    for piece in refs[1:-1]:
        total = total + piece[...]
    rows = total.shape[0]
    refs[-1][0:rows] = total
    refs[-1][rows:] = totals[...]


def cut(pair, at):
    return pair[0][at], pair[1][at]


def query_grad_body(
    block, queries, values, key_high, key_low, key_rest, feat_high, feat_low, grad_numer,
    grad_norm, state_high, state_low, state_rest, logit_ref, grad_weight, score_grad_high, score_grad_low,
):
    rows, width = values.shape
    numer = split(grad_numer[...])
    norm_grad = grad_norm[...]
    scaled_norm = split(norm_grad * (1.0 / width))
    extended = [jnp.concatenate([a, b], axis=1) for a, b in zip(numer, scaled_norm)]
    value_pair = split(values[...])
    feat = (feat_high[...], feat_low[...])
    state = (state_high[...], state_low[...], state_rest[...])
    mask = causal(block)
    parts = []
    for i in range(rows // block):
        at = slice(i * block, (i + 1) * block)
        norm_part = jnp.concatenate([norm_grad[at]] * (block // width), axis=1)
        grad_query = dot5(cut(extended, at), state, NN)
        for j in range(i + 1):
            past = slice(j * block, (j + 1) * block)
            grad_scores = dot3(cut(numer, at), cut(value_pair, past), NT) + norm_part
            if i == j:
                grad_scores = jnp.where(mask, grad_scores, 0.0)
            pair = split(grad_scores)
            score_grad_high[at, past] = pair[0]
            score_grad_low[at, past] = pair[1]
            grad_query = grad_query + dot5(
                pair, (key_high[past], key_low[past], key_rest[past]), NN
            )
        parts.append(logit_grad(joined(cut(feat, at)), grad_query))
    grad_logits = jnp.concatenate(parts, axis=0)
    logit_ref[...] = grad_logits
    grad_weight[...] = dot3(split(queries[...]), split(grad_logits), TN)


def key_inner_body(block, heads, *refs):
    result = refs[-1]
    rows, wide = refs[0].shape
    count = rows // block
    key_sums, value_sums = [None] * count, [None] * count
    for h in range(heads):
        *pairs, grads = refs[7 * h : 7 * h + 7]
        feat, scores, score_grads = pairs[0:2], pairs[2:4], pairs[4:6]
        numer = split(grads[...])
        for i in range(count):
            at = slice(i * block, (i + 1) * block)
            for j in range(i + 1):
                past = slice(j * block, (j + 1) * block)
                pair = (score_grads[0][at, past], score_grads[1][at, past])
                term = dot3(pair, cut(feat, at), TN)
                key_sums[j] = term if key_sums[j] is None else key_sums[j] + term
                pair = (scores[0][at, past], scores[1][at, past])
                term = dot3(pair, cut(numer, at), TN)
                value_sums[j] = term if value_sums[j] is None else value_sums[j] + term
    for j in range(count):
        past = slice(j * block, (j + 1) * block)
        result[past, :wide] = key_sums[j]
        result[past, wide:] = value_sums[j]


def query_out_body(heads, weights, *refs):
    logits, result = refs[:heads], refs[heads]
    width = weights.shape[1]
    for h in range(heads):
        result[:, h * width : (h + 1) * width] = dot3(
            split(logits[h][...]), split(weights[h]), NT
        )


def sum_body(*refs):
    total = refs[0][...]
    for piece in refs[1:-1]:
        total = total + piece[...]
    refs[-1][...] = total


def key_grad_body(share, piece, inner, values, keys, key_high, key_low, *refs):
    logit_ref, state_high, state_low, *parts, scratch, weights = refs
    mine = lax.axis_index("head")
    scratch[...] = jnp.zeros(scratch.shape, F32)
    put_state(piece, scratch, share, mine)
    state = split(scratch[...])
    state_high[...] = state[0]
    state_low[...] = state[1]
    totals = take_totals(piece, share)
    wide = key_high.shape[1]
    grad = dot3(split(values[...]), state, NN) + totals + inner[:, :wide]
    feat = (key_high[...], key_low[...])
    grad_logits = logit_grad(joined(feat), grad)
    logit_ref[...] = grad_logits
    weights[...] = dot3(split(keys[...]), split(grad_logits), TN)
    rows = parts[0].shape[0]
    for m, target in enumerate(parts):
        target[...] = weights[pl.ds(pl.multiple_of((mine ^ m) * rows, 8), rows), :]


def key_out_body(part, logits, inner, state_high, state_low, weight, key_high, key_low, *refs):
    parts, both = refs[:-1], refs[-1]
    mine = lax.axis_index("head")
    width = weight.shape[0]
    wide = key_high.shape[1]
    feat = (key_high[...], key_low[...])
    both[:, :width] = dot3(split(logits[...]), split(weight[...]), NT)
    both[:, width:] = inner[:, wide:] + dot3(feat, (state_high[...], state_low[...]), NT)
    for m, target in enumerate(parts):
        target[...] = both[pl.ds(pl.multiple_of((mine ^ m) * part, 8), part), :]


def key_sum_body(*refs):
    pieces, (grad_key, grad_value) = refs[:-2], refs[-2:]
    total = pieces[0][...]
    for piece in pieces[1:]:
        total = total + piece[...]
    width = grad_key.shape[1]
    grad_key[...] = total[:, :width]
    grad_value[...] = total[:, width:]


def weight_message_body(*refs):
    parts, shard, message = refs[:-2], refs[-2], refs[-1]
    total = parts[0][...]
    for piece in parts[1:]:
        total = total + piece[...]
    rows = total.shape[0]
    message[0:rows] = total
    message[rows:] = shard[...]


def weight_share_body(rows, *refs):
    pieces, share = refs[:-1], refs[-1]
    total = pieces[0][0:rows]
    for piece in pieces[1:]:
        total = total + piece[0:rows]
    share[...] = total


def weight_gather_body(now, rows, *refs):
    pieces, gathered = refs[:-1], refs[-1]
    mine = position(now)
    shard = pieces[0].shape[0] - rows
    for m, piece in enumerate(pieces):
        at = pl.ds(pl.multiple_of((mine ^ m) * shard, 8), shard)
        gathered[at, :] = piece[rows:]


def gather_body(rows, *refs):
    pieces, result = refs[:-1], refs[-1]
    mine = lax.axis_index("head")
    for m, piece in enumerate(pieces):
        result[pl.ds(pl.multiple_of((mine ^ m) * rows, 8), rows), :] = piece[...]


def backward(queries, keys, values, cotangent, source_ids, source_weights, q_feature, k_feature):
    heads, width, half = q_feature.shape
    wide = 2 * half
    rows = queries.shape[0]
    peers = lax.axis_size("head")
    share = width // peers
    part = rows // peers
    block = min(256, rows)
    rising, rising_ups = rounds_of(lax.axis_size("ctx"), peers, True)
    falling, falling_ups = rounds_of(lax.axis_size("ctx"), peers, False)
    message = (2 * share + 8, half)
    bind = functools.partial
    unit = 2 * rows * width * wide
    hbm = pl.BlockSpec(memory_space=pltpu.HBM)

    source_index = lax.broadcasted_iota(jnp.int32, (1, source_weights.shape[0]), 1)
    lookup = source_ids[:, None] == source_index
    weight = jnp.sum(jnp.where(lookup, source_weights[None, :], 0.0), axis=1)
    scaled = cotangent * weight[:, None]

    feat_shape = out((rows, wide), BF16)
    key_high, key_low, key_rest, local = call(
        bind(key_body, share),
        [feat_shape] * 3 + [out(message)],
        [pltpu.with_memory_space_constraint(x, pltpu.HBM) for x in (keys, values, k_feature)],
        6 * unit,
        [hbm] * 3,
        scratch=[
            pltpu.VMEM((width, wide), F32),
            pltpu.VMEM(keys.shape, F32),
            pltpu.VMEM(values.shape, F32),
            pltpu.VMEM(k_feature.shape, F32),
            pltpu.SemaphoreType.DMA((3,)),
        ],
    )

    def neighbor_sum(local, rounds, ups, prefix, weights=()):
        heads_now, kept = 0, None
        held, values = (), local
        for place, now in enumerate(rounds[:-1]):
            received = swap(values, now)
            after = rounds[place + 1]
            tall = message
            final = place + 2 == len(rounds)
            outs, scratch = [out(message)] * (1 if final else 2), []
            extra = ()
            if final and weights:
                heads_now = len(weights)
                shard = heads_now * width // after[2]
                outs.append(out((shard, half)))
                tall = (message[0] + shard, half)
                scratch = [pltpu.VMEM((heads_now * width, half), F32)]
                extra = tuple(weights)
            results = call(
                bind(step_body, now, after, ups, prefix, place == 0, final, heads_now),
                outs + [out(tall)] * (after[2] - 1),
                (local, *held, *received, *extra),
                scratch=scratch,
            )
            keep = 1 if final else 2
            held, results = tuple(results[:keep]), results[keep:]
            if extra:
                kept, results = results[0], results[1:]
            values = results
        received = swap(values, rounds[-1])
        (result,) = call(
            bind(last_body, rounds[-1], ups, prefix), [out(message)], (held[0], *received)
        )
        if kept is None:
            return result, None
        (shard_sum,) = call(bind(shard_sum_body, message[0]), [out(kept.shape)], (kept, *received))
        return result, shard_sum

    before, _ = neighbor_sum(local, rising, rising_ups, True)
    prefix = [before] + exchange(before, peers)

    def query_spec(h):
        return pl.BlockSpec((rows, width), lambda i: (0, h))

    feats, scores, inner = [], [], []
    for h in range(heads):
        args = (queries, q_feature, values, key_high, key_low)
        outs = (
            [feat_shape] * 2 + [out((rows, rows), BF16)] * 2 + [out((rows, width))] * 2
        )
        results = call(
            bind(query_body, block),
            outs,
            args,
            9 * unit,
            [query_spec(h), pl.BlockSpec((1, width, half), lambda i, h=h: (h, 0, 0))]
            + [whole(a.shape) for a in args[2:]],
            [whole(o.shape) for o in outs],
        )
        feats.append(results[0:2])
        scores.append(results[2:4])
        inner.append(results[4:6])

    flat_feats = [x for pair in feats for x in pair]
    results = call(
        bind(carried_body, heads, share),
        [out((rows, width))] * (2 * heads) + [out((2 * share, half))] * peers,
        (before, scaled, *flat_feats, *[pair[1] for pair in inner]),
        6 * heads * unit,
        scratch=[pltpu.VMEM((width, wide), F32)],
    )
    norms, results = results[:heads], results[heads:]
    grads, results = results[:heads], results[heads:]
    carried_parts = [results[0]] + exchange(results[1:], peers)
    results = call(
        bind(inter_body, heads, peers, share),
        [out((2 * width, wide), BF16)] * 3
        + [out((8, half))]
        + [out((rows, width))] * heads,
        (scaled, *prefix, *flat_feats, *[pair[0] for pair in inner], *norms),
        4 * heads * unit,
        scratch=[pltpu.VMEM((width, wide), F32)],
    )
    state, carried_totals, norm_grads = results[:3], results[3], results[4:]
    (carried,) = call(carried_sum_body, [out(message)], (carried_totals, *carried_parts))

    weight_grads, query_logits, inner_args = [], [], []
    for h in range(heads):
        args = [
            queries, values, key_high, key_low, key_rest, *feats[h], grads[h], norm_grads[h],
            *state,
        ]
        outs = [out((rows, half)), out((width, half))] + [out((rows, rows), BF16)] * 2
        logits, grad_weight, *score_grads = call(
            bind(query_grad_body, block),
            outs,
            args,
            8 * unit,
            [query_spec(h)] + [whole(a.shape) for a in args[1:]],
            [whole(o.shape) for o in outs],
        )
        query_logits.append(logits)
        weight_grads.append(grad_weight)
        inner_args += [*feats[h], *scores[h], *score_grads, grads[h]]
    (key_inner,) = call(
        bind(key_inner_body, block, heads),
        [out((rows, wide + width))],
        inner_args,
        6 * heads * unit,
    )
    (grad_queries,) = call(
        bind(query_out_body, heads),
        [out((rows, heads * width))],
        (q_feature, *query_logits),
        3 * unit,
    )

    later, q_shard = neighbor_sum(carried, falling, falling_ups, False, weight_grads)
    shard = q_shard.shape[0]

    weight_rows = width // peers
    results = call(
        bind(key_grad_body, share),
        [out((rows, half))]
        + [out((width, wide), BF16)] * 2
        + [out((weight_rows, half))] * peers,
        (later, key_inner, values, keys, key_high, key_low),
        6 * unit,
        scratch=[pltpu.VMEM((width, wide), F32), pltpu.VMEM((width, half), F32)],
    )
    key_logits, later_high, later_low = results[:3]
    weight_parts = results[3:]
    weight_parts = [weight_parts[0]] + exchange(weight_parts[1:], peers)
    (total,) = call(
        weight_message_body, [out((weight_rows + shard, half))], (*weight_parts, q_shard)
    )
    key_parts = call(
        bind(key_out_body, part),
        [out((part, 2 * width))] * peers,
        (key_logits, key_inner, later_high, later_low, k_feature, key_high, key_low),
        6 * unit,
        scratch=[pltpu.VMEM((rows, 2 * width), F32)],
    )
    key_parts = [key_parts[0]] + exchange(key_parts[1:], peers)
    grad_keys, grad_values = call(key_sum_body, [out((part, width))] * 2, key_parts)
    for now in falling[:-1]:
        received = swap(total, now)
        (total,) = call(sum_body, [out(total.shape)], (total, *received))
    received = swap(total, falling[-1])
    (k_share,) = call(
        bind(weight_share_body, weight_rows), [out((weight_rows, half))], (total, *received)
    )
    shares = [k_share] + exchange(k_share, peers)
    (k_sum,) = call(bind(gather_body, weight_rows), [out((width, half))], shares)
    (q_sum,) = call(
        bind(weight_gather_body, falling[-1], weight_rows),
        [out((heads * width, half))],
        (total, *received),
    )
    return (
        grad_queries,
        grad_keys,
        grad_values,
        q_sum.reshape(heads, width, half),
        k_sum,
    )


def solution(mesh):
    placed = (
        P("ctx", "head"),
        P("ctx", None),
        P("ctx", None),
        P("ctx", "head"),
        P("ctx"),
        P(),
        P("head", None, None),
        P(),
    )
    return jax.shard_map(
        backward,
        mesh=mesh,
        in_specs=placed,
        out_specs=(
            P("ctx", "head"),
            P(("ctx", "head"), None),
            P(("ctx", "head"), None),
            P("head", None, None),
            P(),
        ),
        check_vma=False,
    )
```
